32 devices in a mesh: seq: 2 (over x), mp: 16 (over z, y, core).
Axes of the slice: x: 2, y: 2, z: 4, core: 2. Of those that a mesh axis runs over, the one named last changes fastest.
Arguments:
- tokens: bfloat16 [4096, 2048], P(('seq', 'mp')), may hold values from -6 to 6
- lengths: int32 [2, 3], P('seq'), may hold values from 1 to 1536, 2048 in all within a row
- norm_gains: float32 [2, 2048], replicated, may hold values from 0.5 to 1.5
- norm_biases: float32 [2, 2048], replicated, may hold values from -2 to 2
- w_query: bfloat16 [2048, 2048], P(None, 'mp'), may hold values from -0.125 to 0.125
- w_key: bfloat16 [2048, 2048], P(None, 'mp'), may hold values from -0.125 to 0.125
- w_value: bfloat16 [2048, 4096], P(None, 'mp'), may hold values from -0.125 to 0.125
- w_gate: bfloat16 [2048, 4096], P(None, 'mp'), may hold values from -0.125 to 0.125
- w_out: bfloat16 [4096, 2048], P('mp'), may hold values from -0.125 to 0.125
- w_up: bfloat16 [2048, 4096], P(None, 'mp'), may hold values from -0.125 to 0.125
- w_down: bfloat16 [4096, 2048], P('mp'), may hold values from -0.125 to 0.125
- out_grad: bfloat16 [4096, 2048], P(('seq', 'mp')), may hold values from -6 to 6
Outputs:
- layer_out: float32 [4096, 2048], P(('seq', 'mp'))
- tokens_grad: float32 [4096, 2048], P(('seq', 'mp'))
- query_grad: float32 [2048, 2048], P(None, 'mp')
- key_grad: float32 [2048, 2048], P(None, 'mp')
- value_grad: float32 [2048, 4096], P(None, 'mp')
- gate_grad: float32 [2048, 4096], P(None, 'mp')
- out_weight_grad: float32 [4096, 2048], P('mp')
- up_grad: float32 [2048, 4096], P(None, 'mp')
- down_grad: float32 [4096, 2048], P('mp')
- gains_grad: float32 [2, 2048], P(None, 'mp')
- biases_grad: float32 [2, 2048], P(None, 'mp')
The draws below stay inside these ranges and needn't reach their ends.
Inputs may be any that keep to these rules, and one draw needn't show every extreme that they name: Each row of lengths lists the 3 sequences of one group in order; they sum to 2048 and the longest is exactly 1536.
All inputs are finite; a program needn't handle non-finite values.
Results may differ from the reference program's by a relative error of at most 0.017.
Values may be sent and summed in bfloat16 or wider, within the bound.
No kernel may reach another device: no remote copies, remote signals or barrier semaphores. Data moves between devices by JAX's collectives and lax.ppermute only.
A program may use at most 576 MiB of HBM per device.

```python
import math
import jax
import jax.numpy as jnp
import numpy as np
from jax import lax

D = 2048
HEADS = 8
KEY = 256
VAL = 512
FF = 4096
SPAN = 512
VALUE = 4096
ROWS = 2048
TOKENS = 4096
SEQS = 3
MAXLEN = 1536
N_SEQ = 2
N_MP = 16


def block_scale(rng, shape, pieces, least, top_value):
    factor_of = 1.0
    for axis_at, parts in pieces:
        steps = jax.random.uniform(jax.random.fold_in(jax.random.fold_in(rng, 6), axis_at), (parts,), jnp.float32, least / len(pieces), top_value / len(pieces))
        factor_of = factor_of * jnp.repeat(jnp.exp(steps), shape[axis_at] // parts).reshape((-1,) + (1,) * (len(shape) - 1 - axis_at))
    return factor_of


def profile(number_of, total, reach, lean):
    loads = [(1 << 20) // math.isqrt(standing ** lean) + 1 for standing in range(2, number_of + 1)]
    surplus, counts = total - reach - (number_of - 1), [1] * (number_of - 1)
    while surplus > 0:
        movable = [i for i in range(number_of - 1) if counts[i] < reach]
        mass, remaining = sum([loads[i] for i in movable]), surplus
        for i in movable:
            extra = min(reach - counts[i], max(1, remaining * loads[i] // mass), surplus)
            counts[i] = counts[i] + extra
            surplus = surplus - extra
    return np.array([reach] + counts)


def uneven(stream_key, count, total, reach, slope):
    if count == 2:
        one = jax.random.randint(stream_key, (), max(1, total - reach), min(reach, total - 1) + 1)
        return jnp.stack([one, total - one])
    sizes = jnp.asarray(profile(count, total, reach, slope), jnp.int32)
    couples = (count - 1) // 2
    donor, taker = sizes[1:1 + 2 * couples:2], sizes[2:2 + 2 * couples:2]
    margin = jnp.minimum(donor - 1, reach - taker)
    shifted = jax.random.randint(jax.random.fold_in(stream_key, 1), (couples,), 0, 1 << 20) % (margin + 1)
    sizes = sizes.at[1:1 + 2 * couples:2].set(donor - shifted).at[2:2 + 2 * couples:2].set(taker + shifted)
    return sizes[jax.random.permutation(jax.random.fold_in(stream_key, 2), count)]


def normal_values(rng, extent, width, limit, split=(), kind=jnp.bfloat16):
    values = width * jax.random.normal(rng, extent, jnp.float32)
    if split:
        values = values * block_scale(rng, extent, split, -0.22, 0.18)
    return jnp.clip(values, -limit, limit).astype(kind)


def setup_inputs(seed: int = 0) -> dict:
    splits = jax.random.split(jax.random.key(seed), 13)
    return {
        "tokens": normal_values(splits[0], (TOKENS, D), 1.0, 6.0, ((0, 32),)),
        "lengths": jax.vmap(lambda own: uneven(own, SEQS, ROWS, MAXLEN, 2))(jax.random.split(splits[1], N_SEQ)).reshape((N_SEQ, SEQS)).astype(jnp.int32),
        "norm_gains": jnp.clip(1.0 + 0.1 * jax.random.normal(splits[2], (2, D), jnp.float32), 0.5, 1.5),
        "norm_biases": normal_values(splits[3], (2, D), 0.3, 2.0, (), jnp.float32),
        "w_query": normal_values(splits[4], (D, HEADS * KEY), D ** -0.5, 0.125, ((1, 16),)),
        "w_key": normal_values(splits[5], (D, HEADS * KEY), D ** -0.5, 0.125, ((1, 16),)),
        "w_value": normal_values(splits[6], (D, VALUE), D ** -0.5, 0.125, ((1, 16),)),
        "w_gate": normal_values(splits[7], (D, VALUE), D ** -0.5, 0.125, ((1, 16),)),
        "w_out": normal_values(splits[8], (VALUE, D), (VALUE // 2) ** -0.5, 0.125, ((0, 16),)),
        "w_up": normal_values(splits[9], (D, FF), D ** -0.5, 0.125, ((1, 16),)),
        "w_down": normal_values(splits[10], (FF, D), (FF // 2) ** -0.5, 0.125, ((0, 16),)),
        "out_grad": normal_values(splits[11], (TOKENS, D), 1.0, 6.0, ((0, 32),)),
    }


highest = lax.Precision.HIGHEST
group_epsilon = 0.25

@jax.custom_vjp
def low(v):
    return lax.optimization_barrier(v.astype(jnp.bfloat16)).astype(jnp.float32)

@jax.custom_vjp
def low_back(v):
    return v

def low_keep(v):
    return (low(v), None)

def low_pass(kept, grad):
    return (grad,)

def back_keep(v):
    return (v, None)

def back_low(kept, grad):
    return (low(grad),)
low.defvjp(low_keep, low_pass)
low_back.defvjp(back_keep, back_low)

def layer_norm(values, norm_gain, norm_bias):
    average = lax.optimization_barrier(jnp.mean(values, axis=-1, keepdims=True))
    centered = values - average
    variance = lax.optimization_barrier(jnp.mean(centered * centered, axis=-1, keepdims=True))
    return centered * lax.rsqrt(variance + 1e-05) * norm_gain + norm_bias

def sequence_info(lengths_row, group_rows):
    lengths_int = lengths_row.astype(jnp.int32)
    sequence_ends = jnp.cumsum(lengths_int, dtype=jnp.int32).astype(jnp.int32)
    sequence_starts = (sequence_ends - lengths_int).astype(jnp.int32)
    row_ids = jnp.arange(group_rows, dtype=jnp.int32)
    member = (row_ids[:, None] >= sequence_starts[None, :]) & (row_ids[:, None] < sequence_ends[None, :])
    labels = jnp.arange(lengths_int.shape[0], dtype=jnp.int32)
    zero_int = jnp.zeros((), jnp.int32)
    segment = lax.optimization_barrier(jnp.sum(jnp.where(member, labels[None, :], zero_int), axis=1, dtype=jnp.int32)).astype(jnp.int32)
    begins = lax.optimization_barrier(jnp.sum(jnp.where(member, sequence_starts[None, :], zero_int), axis=1, dtype=jnp.int32)).astype(jnp.int32)
    position = (row_ids - begins).astype(jnp.int32)
    return (segment, position)

def rotate(values, position, direction):
    half_width = values.shape[-1] // 2
    frequencies = 10000.0 ** (-jnp.arange(half_width).astype(jnp.float32) / half_width)
    angles = position.astype(jnp.float32)[:, None] * frequencies[None, :]
    cosine = jnp.cos(angles)
    sine_part = direction * jnp.sin(angles)
    paired = values.reshape(values.shape[0], half_width, 2)
    even_part = paired[:, :, 0]
    odd_part = paired[:, :, 1]
    turned = jnp.stack([even_part * cosine - odd_part * sine_part, even_part * sine_part + odd_part * cosine], axis=-1)
    return turned.reshape(values.shape)

def span_masks(segment_part, previous, log_decay):
    offsets = jnp.arange(SPAN, dtype=jnp.int32)
    distance = (offsets[:, None] - offsets[None, :]).astype(jnp.int32)
    same_sequence = (distance >= 0) & (segment_part[:, None] == segment_part[None, :])
    safe_distance = jnp.where(same_sequence, distance, jnp.zeros_like(distance)).astype(jnp.float32)
    decayed = jnp.exp(safe_distance * log_decay)
    weights = jnp.where(same_sequence, decayed, jnp.zeros_like(decayed))
    carry_decay = jnp.exp((offsets + 1).astype(jnp.float32) * log_decay)
    carried = jnp.where(segment_part == previous, carry_decay, jnp.zeros_like(carry_decay))
    last_segment = segment_part[-1]
    block_decay = jnp.exp(jnp.float32(SPAN) * log_decay)
    keep_factor = jnp.where(previous == last_segment, block_decay, jnp.zeros_like(block_decay))
    fresh_decay = jnp.exp((SPAN - 1 - offsets).astype(jnp.float32) * log_decay)
    fresh_weights = jnp.where(segment_part == last_segment, fresh_decay, jnp.zeros_like(fresh_decay))
    return (weights, carried, keep_factor, fresh_weights, last_segment)

def retain(queries, key_rows, value_rows, segment, log_decay):
    blocks = ROWS // SPAN
    columns = value_rows.shape[1]

    def advance(carry_pair, inputs):
        carry_state, previous = carry_pair
        query_part, key_part, value_part, segment_part = inputs
        weights, carried, keep_factor, fresh_weights, last_segment = span_masks(segment_part, previous, log_decay)
        scores = low_back(jnp.dot(query_part, key_part.T, precision=highest))
        intra_weights = low(scores * weights)
        inner_part = jnp.dot(intra_weights, value_part, precision=highest)
        outer_part = jnp.dot(query_part * carried[:, None], carry_state, precision=highest)
        update = jnp.dot((key_part * fresh_weights[:, None]).T, value_part, precision=highest)
        return ((keep_factor * carry_state + update, last_segment.astype(jnp.int32)), inner_part + outer_part)
    start_pair = (jnp.zeros((KEY, columns), jnp.float32), jnp.full((), -1, jnp.int32))
    inputs = (queries.reshape(blocks, SPAN, KEY), key_rows.reshape(blocks, SPAN, KEY), value_rows.reshape(blocks, SPAN, columns), segment.reshape(blocks, SPAN).astype(jnp.int32))
    unused, outputs = lax.scan(jax.checkpoint(advance), start_pair, inputs)
    return outputs.reshape(ROWS, columns)

def group_forward(tokens_group, lengths_row, norm_gains, norm_biases, w_query, w_key, w_value, w_gate, w_out, w_up, w_down):
    segment, position = sequence_info(lengths_row, ROWS)
    per_head = N_MP // HEADS
    columns = VALUE // N_MP
    key_scale = KEY ** (-0.5)
    normed_one = low(layer_norm(tokens_group, norm_gains[0], norm_biases[0]))
    query_pre = jnp.dot(normed_one, w_query, precision=highest)
    key_pre = jnp.dot(normed_one, w_key, precision=highest)
    value_rows = low(low_back(jnp.dot(normed_one, w_value, precision=highest)))
    gate_pre = low_back(jnp.dot(normed_one, w_gate, precision=highest))
    query_heads = jnp.repeat(query_pre.reshape(ROWS, HEADS, KEY).transpose(1, 0, 2), per_head, axis=0)
    key_heads = jnp.repeat(key_pre.reshape(ROWS, HEADS, KEY).transpose(1, 0, 2), per_head, axis=0)
    value_blocks = value_rows.reshape(ROWS, N_MP, columns).transpose(1, 0, 2)
    decays = jnp.repeat(jnp.log(1.0 - 2.0 ** (-5.0 - jnp.arange(HEADS).astype(jnp.float32))), per_head)

    def one_block(query_block, key_block, value_block, log_decay):
        queries = low(rotate(low_back(query_block), position, 1.0))
        key_rows = low(rotate(low_back(key_block), position, 1.0) * key_scale)
        return retain(queries, key_rows, value_block, segment, log_decay)
    retained = low_back(jax.vmap(one_block)(query_heads, key_heads, value_blocks, decays))
    shaped = retained.reshape(HEADS, per_head, ROWS, columns)
    totals = lax.optimization_barrier(jnp.sum(shaped, axis=(1, 3), keepdims=True))
    squares = lax.optimization_barrier(jnp.sum(shaped * shaped, axis=(1, 3), keepdims=True))
    average = totals / VAL
    grouped = (shaped - average) * lax.rsqrt(squares / VAL - average * average + group_epsilon)
    grouped = grouped.transpose(2, 0, 1, 3).reshape(ROWS, VALUE)
    gated = low(jax.nn.silu(gate_pre) * grouped)
    middle = tokens_group + low_back(jnp.dot(gated, w_out, precision=highest))
    normed_two = low(layer_norm(middle, norm_gains[1], norm_biases[1]))
    hidden = low_back(jnp.dot(normed_two, w_up, precision=highest))
    active = low(jax.nn.gelu(hidden, approximate=False))
    return middle + low_back(jnp.dot(active, w_down, precision=highest))

def forward(tokens, lengths, norm_gains, norm_biases, w_query, w_key, w_value, w_gate, w_out, w_up, w_down):
    outputs = []
    for group_index in range(N_SEQ):
        tokens_group = tokens[group_index * ROWS:(group_index + 1) * ROWS]
        outputs.append(group_forward(tokens_group, lengths[group_index], norm_gains, norm_biases, w_query, w_key, w_value, w_gate, w_out, w_up, w_down))
    return jnp.concatenate(outputs, axis=0)

def reference(tokens, lengths, norm_gains, norm_biases, w_query, w_key, w_value, w_gate, w_out, w_up, w_down, out_grad):

    def layer(tokens_in, gains_in, biases_in, query_in, key_in, value_in, gate_in, out_in, up_in, down_in):
        return forward(tokens_in, lengths, gains_in, biases_in, query_in, key_in, value_in, gate_in, out_in, up_in, down_in)
    primals = (tokens.astype(jnp.float32), norm_gains.astype(jnp.float32), norm_biases.astype(jnp.float32), w_query.astype(jnp.float32), w_key.astype(jnp.float32), w_value.astype(jnp.float32), w_gate.astype(jnp.float32), w_out.astype(jnp.float32), w_up.astype(jnp.float32), w_down.astype(jnp.float32))
    layer_out, pullback = jax.vjp(layer, *primals)
    grads = pullback(out_grad.astype(jnp.float32))
    return (layer_out, grads[0], grads[3], grads[4], grads[5], grads[6], grads[7], grads[8], grads[9], grads[1], grads[2])
```

```python
import jax
import jax.numpy as jnp
import numpy as np
from jax import lax
from jax.sharding import PartitionSpec as P

HEADS = 8
KEY = 256
VAL = 512

epsilon = 1e-05
group_epsilon = 0.25

RING = tuple(range(0, HEADS, 2)) + tuple(range(HEADS - 1, 0, -2))
ARRIVAL = ((0,), (-1, 1), (-2, 2), (-3, 3), (4,))
OFFSETS = tuple(offset for batch in ARRIVAL for offset in batch)


def contract(left_side, right_side, left_dim, right_dim):
    return lax.dot_general(
        left_side,
        right_side,
        (((left_dim,), (right_dim,)), ((), ())),
        preferred_element_type=jnp.float32,
    )


def row_stats(values):
    average = jnp.mean(values, axis=-1, keepdims=True)
    centered = values - average
    variance = jnp.mean(centered * centered, axis=-1, keepdims=True)
    return average, lax.rsqrt(variance + epsilon)


def normalize_back(grad_normed, unit_rows, inverse, norm_gain):
    scaled = grad_normed * norm_gain
    plain_mean = jnp.mean(scaled, axis=-1, keepdims=True)
    cross_mean = jnp.mean(scaled * unit_rows, axis=-1, keepdims=True)
    return inverse * (scaled - plain_mean - unit_rows * cross_mean)


def gelu_slope(hidden):
    cumulative = 0.5 * (1.0 + lax.erf(hidden * 0.7071067811865476))
    density = jnp.exp(-0.5 * hidden * hidden) * 0.3989422804014327
    return cumulative + hidden * density


def turn(values, cosine, sine):
    half = values.shape[-1] // 2
    even, odd = values[:, :half], values[:, half:]
    return jnp.concatenate([even * cosine - odd * sine, even * sine + odd * cosine], axis=1)


def local(
    tokens,
    lengths,
    norm_gains,
    norm_biases,
    w_query,
    w_key,
    w_value,
    w_gate,
    w_out,
    w_up,
    w_down,
    out_grad,
):
    bf16, f32 = jnp.bfloat16, jnp.float32
    mp_size = lax.axis_size("mp")
    seq_size = lax.axis_size("seq")
    ranks = mp_size // HEADS
    mp_index = lax.axis_index("mp")
    head = mp_index // ranks
    rank = mp_index % ranks
    chunk = tokens.shape[0]
    width = tokens.shape[1]
    half = width // 2
    own_rows = chunk * HEADS
    key_scale = KEY ** (-0.5)

    def ring_shift(value, step):
        pairs = [
            (RING[k] * ranks + r, RING[(k + step) % HEADS] * ranks + r)
            for k in range(HEADS)
            for r in range(ranks)
        ]
        return lax.ppermute(value, "mp", pairs)

    def rank_shift(value, by):
        pairs = [(h * ranks + r, h * ranks + (r + by) % ranks) for h in range(HEADS) for r in range(ranks)]
        return lax.ppermute(value, "mp", pairs)

    def gather_ring(block):
        forth, back = block, block
        batches = [block]
        for _ in range(3):
            forth, back = ring_shift(forth, 1), ring_shift(back, -1)
            batches.append(jnp.concatenate([forth, back], axis=0))
        left = ring_shift(forth[:, :half], 1)
        right = ring_shift(back[:, half:], -1)
        batches.append(jnp.concatenate([left, right], axis=1))
        return batches

    def scatter_ring(parts):
        far = parts[4].astype(bf16)
        forth = ring_shift(far[:, :half], 1).astype(f32)
        back = ring_shift(far[:, half:], -1).astype(f32)
        for at in (3, 2, 1):
            back_part, forth_part = parts[at][:chunk], parts[at][chunk:]
            if at == 3:
                forth = jnp.concatenate([forth_part[:, :half] + forth, forth_part[:, half:]], axis=1)
                back = jnp.concatenate([back_part[:, :half], back_part[:, half:] + back], axis=1)
            else:
                forth = forth_part + forth
                back = back_part + back
            forth = ring_shift(forth.astype(bf16), 1).astype(f32)
            back = ring_shift(back.astype(bf16), -1).astype(f32)
        return parts[0] + forth + back

    def assemble(shard, axis):
        pieces = [shard] + [rank_shift(shard, t) for t in range(1, ranks)]
        ordered = []
        for spot in range(ranks):
            value = pieces[0]
            for t in range(1, ranks):
                value = jnp.where((rank - t + ranks) % ranks == spot, pieces[t], value)
            ordered.append(value)
        return jnp.concatenate(ordered, axis=axis)

    def place(buffer, piece, first):
        return lax.dynamic_update_slice(buffer, piece, (first, 0))

    first_row = []
    at = 0
    for batch in ARRIVAL:
        first_row.append(at)
        at += chunk * len(batch)

    def batch_of(array, at):
        return array[first_row[at] : first_row[at] + chunk * len(ARRIVAL[at])]

    table = np.zeros((HEADS, HEADS), np.int32)
    for k, h in enumerate(RING):
        for j, offset in enumerate(OFFSETS):
            table[h, j] = RING[(k + offset) % HEADS]
    sources = lax.dynamic_slice_in_dim(jnp.asarray(table), head, 1, 0)[0]
    inner = jnp.arange(chunk, dtype=jnp.int32)
    row_ids = jnp.concatenate(
        [
            (((sources * ranks + (rank - t + ranks) % ranks) * chunk)[:, None] + inner[None, :]).reshape(-1)
            for t in range(ranks)
        ]
    )
    ends = jnp.cumsum(lengths[0], dtype=jnp.int32)
    starts = ends - lengths[0]
    member = (row_ids[:, None] >= starts[None, :]) & (row_ids[:, None] < ends[None, :])
    begins = jnp.sum(jnp.where(member, starts[None, :], 0), axis=1, dtype=jnp.int32)
    position = (row_ids - begins)[:own_rows]
    frequencies = 10000.0 ** (-jnp.arange(KEY // 2).astype(f32) / (KEY // 2))
    angles = position.astype(f32)[:, None] * frequencies[None, :]
    cosine, sine = jnp.cos(angles), jnp.sin(angles)
    log_decay = jnp.log(1.0 - 2.0 ** (-5.0 - head.astype(f32)))

    def decay_of(distance, allowed):
        allowed = allowed & (distance >= 0)
        safe = jnp.where(allowed, distance, 0).astype(f32)
        return jnp.where(allowed, jnp.exp(safe * log_decay), 0.0)

    def query_decay(at):
        ids, first = batch_of(row_ids, at), batch_of(begins, at)
        return decay_of(ids[:, None] - row_ids[None, :], row_ids[None, :] >= first[:, None])

    def key_decay(at):
        ids = batch_of(row_ids, at)
        return decay_of(row_ids[None, :] - ids[:, None], ids[:, None] >= begins[None, :])

    with jax.named_scope("gather_tokens"):
        token_batches = gather_ring(tokens)
    with jax.named_scope("head_weights"):
        split = np.zeros((KEY, KEY), np.float32)
        for i in range(KEY // 2):
            split[2 * i, i] = 1.0
            split[2 * i + 1, KEY // 2 + i] = 1.0
        split = jnp.asarray(split, bf16)

        def separate(weight):
            return jnp.dot(weight, split, preferred_element_type=f32).astype(bf16)

        def interleave(grads):
            return contract(grads, split, 1, 1).astype(bf16)

        in_weights = jnp.concatenate(
            [
                separate(assemble(w_query, 1)),
                separate(assemble(w_key, 1)),
                assemble(w_value, 1),
                assemble(w_gate, 1),
            ],
            axis=1,
        )
        out_weight = assemble(w_out, 0)
        up_weight = assemble(w_up, 1)
        down_weight = assemble(w_down, 0)

    all_qkv = jnp.zeros((ranks * own_rows, 2 * KEY + VAL), bf16)
    rows_one = jnp.zeros((own_rows, width), bf16)
    gate_pre, stats_one = [], []
    with jax.named_scope("project_in"):
        for at in range(5):
            raw = token_batches[at].astype(f32)
            average, inverse = row_stats(raw)
            stats_one.append((average, inverse))
            normed = ((raw - average) * inverse * norm_gains[0] + norm_biases[0]).astype(bf16)
            rows_one = place(rows_one, normed, first_row[at])
            out = jnp.dot(normed, in_weights, preferred_element_type=f32)
            c, s = batch_of(cosine, at), batch_of(sine, at)
            qkv = jnp.concatenate(
                [
                    turn(out[:, :KEY], c, s),
                    turn(out[:, KEY : 2 * KEY], c, s) * key_scale,
                    out[:, 2 * KEY : 2 * KEY + VAL],
                ],
                axis=1,
            ).astype(bf16)
            gate_pre.append(out[:, 2 * KEY + VAL :])
            all_qkv = place(all_qkv, qkv, first_row[at])
            for t in range(1, ranks):
                all_qkv = place(all_qkv, rank_shift(qkv, t), t * own_rows + first_row[at])
    all_q, all_k, all_v = all_qkv[:, :KEY], all_qkv[:, KEY : 2 * KEY], all_qkv[:, 2 * KEY :]

    with jax.named_scope("gather_out_grad"):
        grad_batches = gather_ring(lax.optimization_barrier((out_grad, token_batches[4]))[0])

    grouped, inverse_group, swish = [None] * 5, [None] * 5, [None] * 5
    parts = [None] * 5
    gated_rows = [None] * 5
    with jax.named_scope("retention"):
        for at in (4, 3, 2, 1, 0):
            scores = contract(batch_of(all_q, at), all_k, 1, 1)
            intra = (scores * query_decay(at)).astype(bf16)
            retained = jnp.dot(intra, all_v, preferred_element_type=f32)
            average = jnp.mean(retained, axis=1, keepdims=True)
            square = jnp.mean(retained * retained, axis=1, keepdims=True)
            inverse_group[at] = lax.rsqrt(square - average * average + group_epsilon)
            grouped[at] = (retained - average) * inverse_group[at]
            swish[at] = jax.nn.silu(gate_pre[at])
            gated_rows[at] = (swish[at] * grouped[at]).astype(bf16)
            parts[at] = jnp.dot(gated_rows[at], out_weight, preferred_element_type=f32)
    with jax.named_scope("scatter_branch"):
        middle = tokens.astype(f32) + scatter_ring(parts)

    with jax.named_scope("norm_two"):
        average, inverse_two = row_stats(middle)
        unit_two = (middle - average) * inverse_two
        normed_two = (unit_two * norm_gains[1] + norm_biases[1]).astype(bf16)
    with jax.named_scope("gather_two"):
        two_batches = gather_ring(normed_two)
    down_parts, up_parts = [None] * 5, [None] * 5
    active_rows, grad_hidden_rows = [None] * 5, [None] * 5
    with jax.named_scope("feed_forward"):
        for at in range(5):
            hidden = jnp.dot(two_batches[at], up_weight, preferred_element_type=f32)
            active_rows[at] = jax.nn.gelu(hidden, approximate=False).astype(bf16)
            grad_active = contract(grad_batches[at], down_weight, 1, 1)
            grad_hidden_rows[at] = (grad_active * gelu_slope(hidden)).astype(bf16)
            up_parts[at] = contract(grad_hidden_rows[at], up_weight, 1, 1)
            down_parts[at] = jnp.dot(active_rows[at], down_weight, preferred_element_type=f32)
    with jax.named_scope("scatter_up"):
        grad_normed_two = scatter_ring(up_parts)
    with jax.named_scope("norm_two_back"):
        grad_middle = out_grad.astype(f32) + normalize_back(
            grad_normed_two, unit_two, inverse_two, norm_gains[1]
        )
        grad_branch = grad_middle.astype(bf16)
        gain_two = jnp.sum(grad_normed_two * unit_two, axis=0)
        bias_two = jnp.sum(grad_normed_two, axis=0)
    with jax.named_scope("gather_branch"):
        branch_batches = gather_ring(grad_branch)
    with jax.named_scope("scatter_down"):
        gate = lax.optimization_barrier((down_parts[4], grad_branch))[0]
        layer_out = middle + scatter_ring(down_parts[:4] + [gate])

    all_grad = jnp.zeros((ranks * own_rows, VAL), bf16)
    grad_gate, grad_query = [None] * 5, [None] * 5
    with jax.named_scope("retention_back_rows"):
        for at in range(5):
            grad_gated = contract(branch_batches[at], out_weight, 1, 1)
            pre = gate_pre[at]
            sigmoid = jax.nn.sigmoid(pre)
            grad_gate[at] = (
                grad_gated * grouped[at] * (sigmoid * (1.0 + pre * (1.0 - sigmoid)))
            ).astype(bf16)
            grad_grouped = grad_gated * swish[at]
            plain = jnp.mean(grad_grouped, axis=1, keepdims=True)
            cross = jnp.mean(grad_grouped * grouped[at], axis=1, keepdims=True)
            grad_retained = (
                inverse_group[at] * (grad_grouped - plain - grouped[at] * cross)
            ).astype(bf16)
            all_grad = place(all_grad, grad_retained, first_row[at])
            for t in range(1, ranks):
                all_grad = place(all_grad, rank_shift(grad_retained, t), t * own_rows + first_row[at])
            grad_scores = (contract(grad_retained, all_v, 1, 1) * query_decay(at)).astype(bf16)
            turned = jnp.dot(grad_scores, all_k, preferred_element_type=f32)
            grad_query[at] = turn(turned, batch_of(cosine, at), -batch_of(sine, at)).astype(bf16)
    in_parts = [None] * 5
    grad_key, grad_value = [None] * 5, [None] * 5
    gain_one, bias_one = jnp.zeros((width,), f32), jnp.zeros((width,), f32)
    with jax.named_scope("retention_back_columns"):
        for at in (4, 3, 2, 1, 0):
            weights = key_decay(at)
            intra = (contract(batch_of(all_k, at), all_q, 1, 1) * weights).astype(bf16)
            grad_value[at] = jnp.dot(intra, all_grad, preferred_element_type=f32).astype(bf16)
            grad_scores = (contract(batch_of(all_v, at), all_grad, 1, 1) * weights).astype(bf16)
            turned = jnp.dot(grad_scores, all_q, preferred_element_type=f32)
            grad_key[at] = (
                turn(turned, batch_of(cosine, at), -batch_of(sine, at)) * key_scale
            ).astype(bf16)
            grads = jnp.concatenate([grad_query[at], grad_key[at], grad_value[at], grad_gate[at]], axis=1)
            in_parts[at] = contract(grads, in_weights, 1, 1)
            average, inverse = stats_one[at]
            unit = (token_batches[at].astype(f32) - average) * inverse
            gain_one = gain_one + jnp.sum(in_parts[at] * unit, axis=0)
            bias_one = bias_one + jnp.sum(in_parts[at], axis=0)
    with jax.named_scope("scatter_in"):
        grad_normed_one = scatter_ring(in_parts)
    with jax.named_scope("norm_one_back"):
        average, inverse = stats_one[0]
        unit_one = (tokens.astype(f32) - average) * inverse
        tokens_grad = grad_middle + normalize_back(
            grad_normed_one, unit_one, inverse, norm_gains[0]
        )

    with jax.named_scope("norm_grads"):
        norm_sums = jnp.stack([gain_one, gain_two, bias_one, bias_two])
        total = norm_sums
        for t in range(1, ranks):
            total = total + rank_shift(norm_sums, t)
        for bit in (1, 2, 4):
            pairs = [(h * ranks + r, (h ^ bit) * ranks + r) for h in range(HEADS) for r in range(ranks)]
            total = total + lax.ppermute(total, "mp", pairs)
        columns = width // mp_size
        mine = lax.dynamic_slice_in_dim(total, mp_index * columns, columns, 1)

        def sum_groups(value):
            result = value
            for t in range(1, seq_size):
                pairs = [(i, (i + t) % seq_size) for i in range(seq_size)]
                result = result + lax.ppermute(value, "seq", pairs)
            return result

        mine = sum_groups(mine)

    def weight_shard(left, right, sharded_left):
        source = left if sharded_left else right
        size = source.shape[1] // ranks

        def shard(spot):
            cut = lax.dynamic_slice_in_dim(source, spot * size, size, 1)
            return contract(cut, right, 0, 0) if sharded_left else contract(left, cut, 0, 0)

        result = shard(rank)
        for t in range(1, ranks):
            result = result + rank_shift(shard((rank + t) % ranks).astype(bf16), t).astype(f32)
        return sum_groups(result.astype(bf16)).astype(f32)

    def rows(batches):
        return jnp.concatenate(batches, axis=0)

    with jax.named_scope("down_grad"):
        out_grad_rows = rows(grad_batches)
        down_grad = weight_shard(rows(active_rows), out_grad_rows, True)
    with jax.named_scope("up_grad"):
        up_grad = weight_shard(rows(two_batches), rows(grad_hidden_rows), False)
    with jax.named_scope("out_weight_grad"):
        out_weight_grad = weight_shard(rows(gated_rows), rows(branch_batches), True)
    with jax.named_scope("gate_grad"):
        gate_grad = weight_shard(rows_one, rows(grad_gate), False)
    with jax.named_scope("query_grad"):
        query_grad = weight_shard(rows_one, interleave(rows(grad_query)), False)
    with jax.named_scope("value_grad"):
        value_grad = weight_shard(rows_one, rows(grad_value), False)
    with jax.named_scope("key_grad"):
        key_grad = weight_shard(rows_one, interleave(rows(grad_key)), False)
    return (
        layer_out,
        tokens_grad,
        query_grad,
        key_grad,
        value_grad,
        gate_grad,
        out_weight_grad,
        up_grad,
        down_grad,
        mine[:2],
        mine[2:],
    )


def solution(mesh):
    return jax.shard_map(
        local,
        mesh=mesh,
        in_specs=(
            P(("seq", "mp"), None),
            P("seq", None),
            P(),
            P(),
            P(None, "mp"),
            P(None, "mp"),
            P(None, "mp"),
            P(None, "mp"),
            P("mp", None),
            P(None, "mp"),
            P("mp", None),
            P(("seq", "mp"), None),
        ),
        out_specs=(
            P(("seq", "mp"), None),
            P(("seq", "mp"), None),
            P(None, "mp"),
            P(None, "mp"),
            P(None, "mp"),
            P(None, "mp"),
            P("mp", None),
            P(None, "mp"),
            P("mp", None),
            P(None, "mp"),
            P(None, "mp"),
        ),
        check_vma=False,
    )
```

```python
import jax
import jax.numpy as jnp
import numpy as np
from jax import lax
from jax.experimental import pallas as pl
from jax.experimental.pallas import tpu as pltpu
from jax.sharding import PartitionSpec as P

HEADS = 8
KEY = 256
VAL = 512
QKV = 2 * KEY + VAL
VMEM_BYTES = 44 << 20

epsilon = 1e-05
group_epsilon = 0.25
key_scale = KEY ** (-0.5)
bf16, f32 = jnp.bfloat16, jnp.float32

RING = tuple(range(0, HEADS, 2)) + tuple(range(HEADS - 1, 0, -2))
BATCHES = ((0, -1, 1, -2, 2), (-3, 3), (4,))
OFFSETS = tuple(offset for batch in BATCHES for offset in batch)
FIRST = (0, 5, 7)


def contract(left_side, right_side, left_dim, right_dim):
    return lax.dot_general(
        left_side,
        right_side,
        (((left_dim,), (right_dim,)), ((), ())),
        preferred_element_type=f32,
    )


def after(value, *earlier):
    return lax.optimization_barrier((value, *earlier))[0]


def row_stats(values):
    average = jnp.mean(values, axis=-1, keepdims=True)
    centered = values - average
    variance = jnp.mean(centered * centered, axis=-1, keepdims=True)
    return average, lax.rsqrt(variance + epsilon)


def normalize_back(grad_normed, unit_rows, inverse, norm_gain):
    scaled = grad_normed * norm_gain
    plain_mean = jnp.mean(scaled, axis=-1, keepdims=True)
    cross_mean = jnp.mean(scaled * unit_rows, axis=-1, keepdims=True)
    return inverse * (scaled - plain_mean - unit_rows * cross_mean)


def turn(values, cosine, sine):
    half = values.shape[-1] // 2
    even, odd = values[:, :half], values[:, half:]
    return jnp.concatenate([even * cosine - odd * sine, even * sine + odd * cosine], axis=1)


def sigmoid(values):
    return 1.0 / (1.0 + jnp.exp(-values))


def run(body, name, outs, scratch, *groups, late=(), flops=0, free=False):
    lists = [list(group) if isinstance(group, (list, tuple)) else [group] for group in groups]
    sizes = [len(group) for group in lists]
    values = [value for group in lists for value in group]
    fixed = len(outs) + len(scratch)

    def kernel(*refs):
        split, at = [], 0
        for size in sizes:
            split.append(refs[at : at + size])
            at += size
        sources = refs[at : at + len(late)]
        at += len(late)
        results = refs[at : at + fixed]
        at += fixed
        copies = [
            pltpu.make_async_copy(source, refs[at + i], refs[at + len(late) + i])
            for i, source in enumerate(sources)
        ]
        for copy in copies:
            copy.start()

        def fetch(i):
            def wait():
                copies[i].wait()
                return refs[at + i]

            return wait

        body(*split, *results, *[fetch(i) for i in range(len(late))])

    whole = pl.BlockSpec(memory_space=pltpu.VMEM)
    moved = sum(value.size * value.dtype.itemsize for value in (*values, *late))
    moved += sum(int(np.prod(shape)) * jnp.dtype(dtype).itemsize for shape, dtype in outs)
    return pl.pallas_call(
        kernel,
        out_shape=[jax.ShapeDtypeStruct(shape, dtype) for shape, dtype in outs],
        in_specs=[whole] * len(values) + [pl.BlockSpec(memory_space=pl.ANY)] * len(late),
        out_specs=[whole] * len(outs),
        scratch_shapes=[pltpu.VMEM(shape, dtype) for shape, dtype in scratch]
        + [pltpu.VMEM(value.shape, value.dtype) for value in late]
        + [pltpu.SemaphoreType.DMA(())] * len(late),
        compiler_params=pltpu.CompilerParams(vmem_limit_bytes=VMEM_BYTES),
        cost_estimate=pl.CostEstimate(flops=flops, transcendentals=0, bytes_accessed=0 if free else moved),
        name=name,
    )(*values, *late)


def each_block(count, block, step):
    def body(i, unused):
        step(pl.multiple_of(i * block, block))
        return unused

    lax.fori_loop(0, count // block, body, 0)


def stage_rows(pieces, rows):
    width = rows.shape[1]
    half = pieces[0].shape[1]
    if half < width:
        rows[:, :half] = pieces[0][...]
        rows[:, half:] = pieces[1][...]
    else:
        chunk = rows.shape[0] // len(pieces)
        for at, piece in enumerate(pieces):
            rows[at * chunk : (at + 1) * chunk, :] = piece[...]


def project_body(pieces, norm, angles, tokens, normed, qkv, gate, stats, weights):
    (norm,), (angles,) = norm, angles
    stage_rows(pieces, tokens)
    count, width = normed.shape

    def normalize(first):
        span = pl.ds(first, 64)
        raw = tokens[span, :].astype(f32)
        average, inverse = row_stats(raw)
        stats[span, :] = jnp.concatenate([average, inverse], axis=1)
        value = (raw - average) * inverse * norm[0:1, :] + norm[1:2, :]
        normed[span, :] = value.astype(bf16)

    each_block(count, 64, normalize)
    weights = weights()
    half = KEY // 2
    cosine, sine = angles[:, :half], angles[:, half:]
    for part in range(2):
        raw = contract(normed[...], weights[:, part * KEY : (part + 1) * KEY], 1, 0)
        turned = turn(raw, cosine, sine)
        qkv[:, part * KEY : (part + 1) * KEY] = (turned * key_scale if part else turned).astype(bf16)
    qkv[:, 2 * KEY :] = contract(normed[...], weights[:, 2 * KEY : QKV], 1, 0).astype(bf16)
    gate[...] = contract(normed[...], weights[:, QKV:], 1, 0)


def decays(columns, rows, away, at, chunk, place, by_query):
    span = slice(at * chunk, (at + 1) * chunk)
    ids, begin = columns[span, 0:1], columns[span, 1:2]
    others, other_begin = rows[0:1, place], rows[1:2, place]
    if by_query:
        mask = (others <= ids) & (others >= begin)
        near = columns[span, 2:3]
    else:
        mask = (others >= ids) & (other_begin <= ids)
        near = columns[span, 3:4]
    return jnp.where(mask, near * away[at : at + 1, place], 0.0)


def spans_of(arrays):
    at = 0
    for array in arrays:
        yield array, slice(at, at + array.shape[0])
        at += array.shape[0]


def branch_body(own, every, gate, columns, rows, away, *refs):
    (own,), (gate,), (columns,), (rows,), (away,) = own, gate, columns, rows, away
    *parts, gated, grouped, inverse, intra, out_weight = refs
    count = own.shape[0]
    chunks = away.shape[0]
    chunk = count // chunks
    queries = own[:, :KEY]
    for array, place in spans_of(every):
        scores = contract(queries, array[:, KEY : 2 * KEY], 1, 1)
        for at in range(chunks):
            factor = decays(columns, rows, away, at, chunk, place, True)
            span = slice(at * chunk, (at + 1) * chunk)
            intra[span, place] = (scores[span] * factor).astype(bf16)
    retained = 0.0
    for array, place in spans_of(every):
        retained = retained + contract(intra[:, place], array[:, 2 * KEY :], 1, 0)
    grouped[...] = retained

    def finish(first):
        span = pl.ds(first, 64)
        value = grouped[span, :]
        average = jnp.mean(value, axis=1, keepdims=True)
        square = jnp.mean(value * value, axis=1, keepdims=True)
        scale = lax.rsqrt(square - average * average + group_epsilon)
        inverse[span, :] = scale
        value = (value - average) * scale
        grouped[span, :] = value
        pre = gate[span, :]
        gated[span, :] = (pre * sigmoid(pre) * value).astype(bf16)

    each_block(count, 64, finish)
    store_parts(parts, lambda place, weight=out_weight(): contract(gated[...], weight[:, place], 1, 0))


def store_parts(parts, product):
    first = 0
    for part in parts:
        width = part.shape[1]
        part[...] = product(slice(first, first + width)).astype(bf16)
        first += width


def feed_body(pieces, grad_pieces, rows, grad_rows, active, grad_hidden, *refs):
    *parts, work, up_weight, down_weight = refs
    stage_rows(pieces, rows)
    stage_rows(grad_pieces, grad_rows)
    up_weight = up_weight()
    work[0] = contract(rows[...], up_weight[...], 1, 0)
    work[1] = contract(grad_rows[...], down_weight()[...], 1, 1)

    def finish(first):
        span = pl.ds(first, 32)
        hidden, grad_active = work[0, span, :], work[1, span, :]
        cumulative = 0.5 * (1.0 + lax.erf(hidden * 0.7071067811865476))
        density = jnp.exp(-0.5 * hidden * hidden) * 0.3989422804014327
        active[span, :] = (hidden * cumulative).astype(bf16)
        grad_hidden[span, :] = (grad_active * (cumulative + hidden * density)).astype(bf16)

    each_block(rows.shape[0], 32, finish)
    store_parts(parts, lambda place: contract(grad_hidden[...], up_weight[place, :], 1, 1))


def down_body(active, down_weight, *parts):
    (down_weight,) = down_weight
    for value, targets in zip(active, (parts[:1], parts[1:2], parts[2:])):
        store_parts(targets, lambda place: contract(value[...], down_weight[:, place], 1, 0))


def gate_body(pieces, gate, grouped, inverse, rows, grad_gate, grad_retained, work, out_weight):
    (gate,), (grouped,), (inverse,) = gate, grouped, inverse
    stage_rows(pieces, rows)
    work[...] = contract(rows[...], out_weight()[...], 1, 1)

    def finish(first):
        span = pl.ds(first, 64)
        grad_gated, pre, value = work[span, :], gate[span, :], grouped[span, :]
        sigma = sigmoid(pre)
        grad_gate[span, :] = (grad_gated * value * (sigma * (1.0 + pre * (1.0 - sigma)))).astype(bf16)
        grads = grad_gated * (pre * sigma)
        plain = jnp.mean(grads, axis=1, keepdims=True)
        cross = jnp.mean(grads * value, axis=1, keepdims=True)
        grad_retained[span, :] = (inverse[span, :] * (grads - plain - value * cross)).astype(bf16)

    each_block(rows.shape[0], 64, finish)


def query_body(grads, every, columns, rows, away, angles, split, grad_query, plain_query):
    (grads,), (columns,), (rows,), (away,), (angles,), (split,) = grads, columns, rows, away, angles, split
    chunks = away.shape[0]
    chunk = grads.shape[0] // chunks
    total = 0.0
    for array, place in spans_of(every):
        scores = contract(grads[...], array[:, 2 * KEY :], 1, 1)
        scores = jnp.concatenate(
            [
                (
                    scores[at * chunk : (at + 1) * chunk]
                    * decays(columns, rows, away, at, chunk, place, True)
                ).astype(bf16)
                for at in range(chunks)
            ],
            axis=0,
        )
        total = total + contract(scores, array[:, KEY : 2 * KEY], 1, 0)
    half = KEY // 2
    value = turn(total, angles[:, :half], -angles[:, half:]).astype(bf16)
    grad_query[...] = value
    plain_query[...] = contract(value, split[...], 1, 1).astype(bf16)


def key_body(
    own, every, every_grad, columns, rows, away, angles, split, others, stats,
    grad_key, plain_key, grad_value, sums, *refs,
):
    (own,), (columns,), (rows,), (away,), (angles,), (split,) = own, columns, rows, away, angles, split
    (grad_query, grad_gate), (stats,) = others, stats
    *parts, work, weights, tokens = refs
    chunks = away.shape[0]
    count = own.shape[0]
    chunk = count // chunks
    total_key, total_value = 0.0, 0.0
    for (array, place), grads in zip(spans_of(every), every_grad):
        scores = contract(own[:, KEY : 2 * KEY], array[:, :KEY], 1, 1)
        grad_scores = contract(own[:, 2 * KEY :], grads[...], 1, 1)
        intra, grad_intra = [], []
        for at in range(chunks):
            factor = decays(columns, rows, away, at, chunk, place, False)
            span = slice(at * chunk, (at + 1) * chunk)
            intra.append((scores[span] * factor).astype(bf16))
            grad_intra.append((grad_scores[span] * factor).astype(bf16))
        total_value = total_value + contract(jnp.concatenate(intra, axis=0), grads[...], 1, 0)
        total_key = total_key + contract(jnp.concatenate(grad_intra, axis=0), array[:, :KEY], 1, 0)
    half = KEY // 2
    value = (turn(total_key, angles[:, :half], -angles[:, half:]) * key_scale).astype(bf16)
    grad_key[...] = value
    plain_key[...] = contract(value, split[...], 1, 1).astype(bf16)
    grad_value[...] = total_value.astype(bf16)
    work[:, :KEY] = grad_query[...]
    work[:, KEY : 2 * KEY] = value
    work[:, 2 * KEY : QKV] = grad_value[...]
    work[:, QKV:] = grad_gate[...]
    average, inverse = stats[:, 0:1], stats[:, 1:2]
    weights, tokens = weights(), tokens()
    tile = 512
    first = 0
    for part in parts:
        for at in range(0, part.shape[1], tile):
            place = slice(first + at, first + at + tile)
            value = contract(work[...], weights[place, :], 1, 1)
            part[:, at : at + tile] = value.astype(bf16)
            unit = (tokens[:, place].astype(f32) - average) * inverse
            sums[0:1, place] = jnp.sum(value * unit, axis=0, keepdims=True)
            sums[1:2, place] = jnp.sum(value, axis=0, keepdims=True)
        first += part.shape[1]


def local(
    tokens,
    lengths,
    norm_gains,
    norm_biases,
    w_query,
    w_key,
    w_value,
    w_gate,
    w_out,
    w_up,
    w_down,
    out_grad,
):
    mp_size = lax.axis_size("mp")
    seq_size = lax.axis_size("seq")
    ranks = mp_size // HEADS
    mp_index = lax.axis_index("mp")
    head = mp_index // ranks
    rank = mp_index % ranks
    chunk, width = tokens.shape
    half = width // 2
    own_rows = chunk * HEADS
    sizes = [chunk * len(batch) for batch in BATCHES]

    def ring_shift(value, step):
        pairs = [
            (RING[k] * ranks + r, RING[(k + step) % HEADS] * ranks + r)
            for k in range(HEADS)
            for r in range(ranks)
        ]
        return lax.ppermute(value, "mp", pairs)

    def rank_shift(value, by):
        pairs = [(h * ranks + r, h * ranks + (r + by) % ranks) for h in range(HEADS) for r in range(ranks)]
        return lax.ppermute(value, "mp", pairs)

    def gather_ring(block, work=None, ready=(), hook=None):
        results = []
        hook = hook or (lambda step, pieces: None)

        def use(at, pieces):
            if work:
                results.append(work(at, after(pieces, results[-1:])))

        forth, back = block, block
        near = [block]
        for _ in range(2):
            forth, back = lax.optimization_barrier((ring_shift(forth, 1), ring_shift(back, -1)))
            near += [forth, back]
            hook(len(near) // 2, (forth, back))
        forth, back = after((forth, back), ready)
        forth, back = lax.optimization_barrier((ring_shift(forth, 1), ring_shift(back, -1)))
        hook(3, (forth, back))
        use(0, near)
        far = [forth, back]
        left, right = after((forth[:, :half], back[:, half:]), results)
        left, right = ring_shift(left, 1), ring_shift(right, -1)
        use(1, far)
        ends = list(lax.optimization_barrier((left, right)))
        hook(4, ends)
        use(2, ends)
        return [near, far, ends], results

    def stack(values):
        return values[0] if len(values) == 1 else jnp.concatenate(values, axis=0)

    def scatter_ring(*part_of, hook=None):
        count = len(part_of)
        steps, sends = [], []

        def shift(forth, back):
            forth, back = lax.optimization_barrier((forth, back))
            sends.append((forth, back))
            forth, back = lax.optimization_barrier((ring_shift(forth, 1), ring_shift(back, -1)))
            steps.append((forth, back))
            tie = hook(len(steps), sends[-1], steps[-1]) if hook else None
            forth, back = after((forth, back), tie) if tie is not None else (forth, back)
            forth, back = (
                [value[i * chunk : (i + 1) * chunk].astype(f32) for i in range(count)] for value in (forth, back)
            )
            return forth, back

        far = [part(2, ()) for part in part_of]
        forth, back = shift(stack([value[0] for value in far]), stack([value[1] for value in far]))
        parts = [part(1, sends[0]) for part in part_of]
        forth = stack(
            [
                jnp.concatenate([p[chunk:, :half].astype(f32) + value, p[chunk:, half:].astype(f32)], axis=1)
                for (p,), value in zip(parts, forth)
            ]
        ).astype(bf16)
        back = stack(
            [
                jnp.concatenate([p[:chunk, :half].astype(f32), p[:chunk, half:].astype(f32) + value], axis=1)
                for (p,), value in zip(parts, back)
            ]
        ).astype(bf16)

        def of(value, at):
            return value[at * chunk : (at + 1) * chunk].astype(f32)

        near = None
        for at in (4, 2):
            forth, back = shift(forth, back)
            near = near or [part(0, sends[1])[0] for part in part_of]
            forth = stack([of(p, at) + value for p, value in zip(near, forth)]).astype(bf16)
            back = stack([of(p, at - 1) + value for p, value in zip(near, back)]).astype(bf16)
        forth, back = shift(forth, back)
        return [of(p, 0) + f + b for p, f, b in zip(near, forth, back)], steps

    def collect(shard):
        return [shard] + [rank_shift(shard, t) for t in range(1, ranks)]

    def assemble(pieces, axis):
        ordered = []
        for spot in range(ranks):
            value = pieces[0]
            for t in range(1, ranks):
                value = jnp.where((rank - t + ranks) % ranks == spot, pieces[t], value)
            ordered.append(value)
        return jnp.concatenate(ordered, axis=axis)

    def batch_of(array, at, axis=0):
        first = FIRST[at] * chunk
        return lax.slice_in_dim(array, first, first + sizes[at], axis=axis)

    with jax.named_scope("head_weights"):
        split = np.zeros((KEY, KEY), np.float32)
        for i in range(KEY // 2):
            split[2 * i, i] = 1.0
            split[2 * i + 1, KEY // 2 + i] = 1.0
        split = jnp.asarray(split, bf16)

        def separate(weight):
            return jnp.dot(weight, split, preferred_element_type=f32).astype(bf16)

        query_pieces, key_pieces = collect(w_query), collect(w_key)
        value_pieces = collect(after(w_value, query_pieces[1:]))
        gate_pieces = collect(after(w_gate, key_pieces[1:]))
        in_weights = jnp.concatenate(
            [
                separate(assemble(query_pieces, 1)),
                separate(assemble(key_pieces, 1)),
                assemble(value_pieces, 1),
                assemble(gate_pieces, 1),
            ],
            axis=1,
        )
        out_weight = assemble(collect(after(w_out, value_pieces[1:])), 0)

    with jax.named_scope("row_places"):
        table = np.zeros((HEADS, HEADS), np.int32)
        for k, h in enumerate(RING):
            for j, offset in enumerate(OFFSETS):
                table[h, j] = RING[(k + offset) % HEADS]
        sources = lax.dynamic_slice_in_dim(jnp.asarray(table), head, 1, 0)[0]
        inner = jnp.arange(chunk, dtype=jnp.int32)
        row_ids = jnp.concatenate(
            [
                (((sources * ranks + (rank - t + ranks) % ranks) * chunk)[:, None] + inner[None, :]).reshape(-1)
                for t in range(ranks)
            ]
        )
        ends = jnp.cumsum(lengths[0], dtype=jnp.int32)
        starts = ends - lengths[0]
        member = (row_ids[:, None] >= starts[None, :]) & (row_ids[:, None] < ends[None, :])
        begins = jnp.sum(jnp.where(member, starts[None, :], 0), axis=1, dtype=jnp.int32)
        position = (row_ids - begins)[:own_rows]
        frequencies = 10000.0 ** (-jnp.arange(KEY // 2).astype(f32) / (KEY // 2))
        angles = position.astype(f32)[:, None] * frequencies[None, :]
        angles = jnp.concatenate([jnp.cos(angles), jnp.sin(angles)], axis=1)
        log_decay = jnp.log(1.0 - 2.0 ** (-5.0 - head.astype(f32)))
        bases = row_ids[:own_rows:chunk]
        away = bases[:, None] - row_ids[None, :]
        away_query = jnp.exp(jnp.maximum(away, 1 - chunk).astype(f32) * log_decay)
        away_key = jnp.exp(jnp.maximum(-away, 0).astype(f32) * log_decay)
        near = jnp.tile(inner.astype(f32) * log_decay, HEADS)
        columns = jnp.stack(
            [row_ids[:own_rows].astype(f32), begins[:own_rows].astype(f32), jnp.exp(near), jnp.exp(-near)],
            axis=1,
        )
        rows = jnp.stack([row_ids.astype(f32), begins.astype(f32)])

    def away_of(array, at):
        return array[FIRST[at] : FIRST[at] + len(BATCHES[at])]

    normed_rows, own_qkv, gate_pre, stats_one = [None] * 3, [None] * 3, [None] * 3, [None] * 3
    token_rows = [None] * 3
    norm = jnp.stack([norm_gains[0], norm_biases[0]])

    batch_angles = [batch_of(angles, at) for at in range(3)]
    batch_columns = [batch_of(columns, at) for at in range(3)]
    batch_away = [away_of(away_query, at) for at in range(3)]
    batch_away_key = [away_of(away_key, at) for at in range(3)]
    ready = (in_weights, out_weight, batch_angles, batch_columns, rows, batch_away, batch_away_key, norm)
    ready = lax.optimization_barrier(ready)
    in_weights, out_weight, batch_angles, batch_columns, rows, batch_away, batch_away_key, norm = ready

    def project(at, pieces):
        token_rows[at], normed_rows[at], own_qkv[at], gate_pre[at], stats_one[at] = run(
            project_body,
            "project",
            [
                ((sizes[at], width), bf16),
                ((sizes[at], width), bf16),
                ((sizes[at], QKV), bf16),
                ((sizes[at], VAL), f32),
                ((sizes[at], 2), f32),
            ],
            [],
            pieces,
            norm,
            batch_angles[at],
            late=[in_weights],
            flops=2 * sizes[at] * width * (QKV + VAL),
        )
        return own_qkv[at]

    with jax.named_scope("project_in"):
        token_pieces, _ = gather_ring(tokens, project, ready)
        every_qkv = list(own_qkv)
        for t in range(1, ranks):
            every_qkv += [rank_shift(value, t) for value in own_qkv]
    with jax.named_scope("gather_out_grad"):
        grad_steps = {}
        grad_pieces, _ = gather_ring(after(out_grad, token_pieces[1]), hook=grad_steps.__setitem__)
    with jax.named_scope("feed_weights"):
        up_weight = assemble(collect(after(w_up, token_pieces[2])), 1)
        down_weight = assemble(collect(after(w_down, token_pieces[2])), 0)

    grouped, inverse_group, gated_rows = [None] * 3, [None] * 3, [None] * 3

    def part_shapes(at):
        return [((sizes[at], half), bf16)] * 2 if at == 2 else [((sizes[at], width), bf16)]

    def branch_part(at, earlier):
        *part, gated_rows[at], grouped[at], inverse_group[at] = run(
            branch_body,
            "branch",
            part_shapes(at)
            + [
                ((sizes[at], VAL), bf16),
                ((sizes[at], VAL), f32),
                ((sizes[at], 1), f32),
            ],
            [((sizes[at], ranks * own_rows), bf16)],
            after(own_qkv[at], earlier, grad_steps[2 - at if at < 2 else 1] if at != 1 else ()),
            every_qkv,
            gate_pre[at],
            batch_columns[at],
            rows,
            batch_away[at],
            late=[out_weight],
            flops=2 * sizes[at] * (ranks * own_rows * (KEY + VAL) + VAL * width),
        )
        return part

    with jax.named_scope("retention"):
        (total,), _ = scatter_ring(branch_part)
        middle = tokens.astype(f32) + total

    def shard(left, right, left_sharded, spot):
        cuts = left if left_sharded else right
        cut = cuts.shape[1] // ranks
        piece = lax.dynamic_slice_in_dim(cuts, spot * cut, cut, 1)
        return contract(piece, right, 0, 0) if left_sharded else contract(left, piece, 0, 0)

    def send_shards(left, right, left_sharded):
        others = [shard(left, right, left_sharded, (rank + t) % ranks).astype(bf16) for t in range(1, ranks)]
        return others, [rank_shift(value, t + 1) for t, value in enumerate(others)]

    def own_shard(left, right, left_sharded, arrived):
        result = shard(left, right, left_sharded, rank)
        for value in arrived:
            result = result + value.astype(f32)
        return result.astype(bf16)

    def swap_groups(value, late):
        total = value.astype(f32)
        for t in range(1, seq_size):
            pairs = [(i, (i + t) % seq_size) for i in range(seq_size)]
            total = total + after(lax.ppermute(value, "seq", pairs), late).astype(f32)
        return total

    def joined(batches):
        return jnp.concatenate(batches, axis=0)

    def by_rank(*values):
        cuts = [value.shape[1] // ranks for value in values]
        return jnp.concatenate(
            [value[:, r * cut : (r + 1) * cut] for r in range(ranks) for value, cut in zip(values, cuts)], axis=1
        )

    with jax.named_scope("norm_two"):
        average, inverse_two = row_stats(middle)
        unit_two = (middle - average) * inverse_two
        normed_two = (unit_two * norm_gains[1] + norm_biases[1]).astype(bf16)
    up_parts, two_rows, grad_rows = [None] * 3, [None] * 3, [None] * 3
    active_rows, grad_hidden_rows = [None] * 3, [None] * 3

    def feed(at, pieces):
        two_rows[at], grad_rows[at], active_rows[at], grad_hidden_rows[at], *up_parts[at] = run(
            feed_body,
            "feed",
            [
                ((sizes[at], width), bf16),
                ((sizes[at], width), bf16),
                ((sizes[at], VAL), bf16),
                ((sizes[at], VAL), bf16),
            ]
            + part_shapes(at),
            [((2, sizes[at], VAL), f32)],
            pieces,
            grad_pieces[at],
            late=[up_weight, down_weight],
            flops=6 * sizes[at] * width * VAL,
        )
        return active_rows[at]

    with jax.named_scope("feed_forward"):
        gather_ring(normed_two, feed)
    early = {}

    def up_hook(step, sends, arrived):
        if step == 1:
            with jax.named_scope("down_grad"):
                left, right = joined(after(active_rows, sends)), joined(after(grad_rows, sends))
                early["others"], got = send_shards(left, right, True)
                early["down"] = own_shard(left, right, True, got)
        if step == 2:
            with jax.named_scope("up_grad"):
                left, right = joined(after(two_rows, sends)), joined(after(grad_hidden_rows, sends))
                others, got = send_shards(left, right, False)
                early["up"] = own_shard(left, right, False, got)
        if step == 3:
            with jax.named_scope("down_parts"):
                *parts, left, right = run(
                    down_body,
                    "down",
                    [((size, width), bf16) for size in sizes[:2]] + [((sizes[2], half), bf16)] * 2,
                    [],
                    after(active_rows, sends),
                    down_weight,
                    flops=2 * own_rows * width * VAL,
                )
                early["parts"] = [[value] for value in parts] + [[left, right]]

    with jax.named_scope("scatter_up"):
        (grad_normed_two,), up_steps = scatter_ring(lambda at, earlier: up_parts[at], hook=up_hook)
    down_own, up_own, down_parts = early["down"], early["up"], early["parts"]
    with jax.named_scope("norm_two_back"):
        grad_middle = out_grad.astype(f32) + normalize_back(
            grad_normed_two, unit_two, inverse_two, norm_gains[1]
        )
        grad_branch = grad_middle.astype(bf16)
        gain_two = jnp.sum(grad_normed_two * unit_two, axis=0)
        bias_two = jnp.sum(grad_normed_two, axis=0)

    branch_rows, grad_gate, own_grad = [None] * 3, [None] * 3, [None] * 3
    grad_query, plain_query = [None] * 3, [None] * 3

    def gate_back(at, pieces):
        branch_rows[at], grad_gate[at], own_grad[at] = run(
            gate_body,
            "gate_back",
            [
                ((sizes[at], width), bf16),
                ((sizes[at], VAL), bf16),
                ((sizes[at], VAL), bf16),
            ],
            [((sizes[at], VAL), f32)],
            pieces,
            gate_pre[at],
            grouped[at],
            inverse_group[at],
            late=[out_weight],
            flops=2 * sizes[at] * width * VAL,
        )
        return own_grad[at]

    with jax.named_scope("gate_back"):
        branch_pieces, _ = gather_ring(after(grad_branch, down_own, up_own, down_parts), gate_back)
        every_grad = list(own_grad)
        for t in range(1, ranks):
            every_grad += [rank_shift(value, t) for value in own_grad]
    with jax.named_scope("down_grad"):
        down_grad = swap_groups(down_own, branch_pieces[2])

    def query_back(at, earlier):
        with jax.named_scope("query_back"):
            grad_query[at], plain_query[at] = run(
                query_body,
                "query_back",
                [((sizes[at], KEY), bf16)] * 2,
                [],
                after(own_grad[at], earlier),
                every_qkv,
                batch_columns[at],
                rows,
                batch_away[at],
                batch_angles[at],
                split,
                free=True,
            )

    with jax.named_scope("out_grad"):
        out_sides = joined(gated_rows), joined(branch_rows), True
        out_others, out_got = send_shards(*out_sides)
    late_own = {}
    grad_value, plain_key = [None] * 3, [None] * 3
    norm_sums = []

    def in_part(at, earlier):
        if at == 2:
            query_back(at, out_others)
        if at == 1:
            with jax.named_scope("out_grad"):
                left, right, _ = after(out_sides, earlier)
                late_own["out"] = own_shard(left, right, True, out_got)
            with jax.named_scope("gate_grad"):
                sides = joined(normed_rows), joined(after(grad_gate, late_own["out"])), False
                others, got = send_shards(*sides)
            query_back(at, others)
        if at == 0:
            query_back(at, earlier)
            with jax.named_scope("gate_grad"):
                left, right, _ = after(late_own["sides"], earlier)
                late_own["gate"] = own_shard(left, right, False, late_own["got"])
        if at == 1:
            late_own["sides"], late_own["got"] = sides, got
        _, plain_key[at], grad_value[at], sums, *part = run(
            key_body,
            "key_back",
            [
                ((sizes[at], KEY), bf16),
                ((sizes[at], KEY), bf16),
                ((sizes[at], VAL), bf16),
                ((2, width), f32),
            ]
            + part_shapes(at),
            [((sizes[at], QKV + VAL), bf16)],
            after(own_qkv[at], earlier),
            every_qkv,
            every_grad,
            batch_columns[at],
            rows,
            batch_away_key[at],
            batch_angles[at],
            split,
            [grad_query[at], grad_gate[at]],
            stats_one[at],
            late=[in_weights, token_rows[at]],
            free=True,
        )
        norm_sums.append(sums)
        return part

    with jax.named_scope("key_back"):
        def in_hook(step, sends, arrived):
            if step == 4:
                late_own["end"] = sends
            if step != 3:
                return None
            with jax.named_scope("query_key_value_grad"):
                columns_last = by_rank(joined(grad_value), joined(plain_query), joined(plain_key))
                sides = late_own["sides"][0], columns_last, False
                others, got = send_shards(*sides)
                late_own["last"] = own_shard(*sides, got)
            return late_own["last"]

        (grad_normed_one, total), in_steps = scatter_ring(
            in_part, lambda at, earlier: down_parts[at], hook=in_hook
        )
        layer_out = middle + total
    with jax.named_scope("norm_one_back"):
        tokens_grad = grad_middle + normalize_back(
            grad_normed_one,
            (tokens.astype(f32) - stats_one[0][:chunk, 0:1]) * stats_one[0][:chunk, 1:2],
            stats_one[0][:chunk, 1:2],
            norm_gains[0],
        )

    def sum_groups(value):
        result = value
        for t in range(1, seq_size):
            pairs = [(i, (i + t) % seq_size) for i in range(seq_size)]
            result = result + lax.ppermute(value, "seq", pairs)
        return result

    with jax.named_scope("norm_grads"):
        gain_one, bias_one = sum(norm_sums)
        total_sums = jnp.stack([gain_one, gain_two, bias_one, bias_two])
        total_sums = after(total_sums, late_own["end"])
        total = total_sums
        for t in range(1, ranks):
            total = total + rank_shift(total_sums, t)
        for bit in (1, 2, 4):
            pairs = [(h * ranks + r, (h ^ bit) * ranks + r) for h in range(HEADS) for r in range(ranks)]
            total = total + lax.ppermute(total, "mp", pairs)
        span = width // mp_size
        mine = sum_groups(lax.dynamic_slice_in_dim(total, mp_index * span, span, 1))

    with jax.named_scope("up_grad"):
        up_grad = swap_groups(up_own, in_steps[0])
    with jax.named_scope("out_grad"):
        out_weight_grad = swap_groups(late_own["out"], in_steps[2])
    with jax.named_scope("gate_grad"):
        gate_grad = swap_groups(late_own["gate"], late_own["end"])
    with jax.named_scope("query_key_value_grad"):
        last = swap_groups(late_own["last"], in_steps[3])
        value_end, query_end = VAL // ranks, (VAL + KEY) // ranks
        value_grad, query_grad, key_grad = last[:, :value_end], last[:, value_end:query_end], last[:, query_end:]
    return (
        layer_out,
        tokens_grad,
        query_grad,
        key_grad,
        value_grad,
        gate_grad,
        out_weight_grad,
        up_grad,
        down_grad,
        mine[:2],
        mine[2:],
    )


def solution(mesh):
    return jax.shard_map(
        local,
        mesh=mesh,
        in_specs=(
            P(("seq", "mp"), None),
            P("seq", None),
            P(),
            P(),
            P(None, "mp"),
            P(None, "mp"),
            P(None, "mp"),
            P(None, "mp"),
            P("mp", None),
            P(None, "mp"),
            P("mp", None),
            P(("seq", "mp"), None),
        ),
        out_specs=(
            P(("seq", "mp"), None),
            P(("seq", "mp"), None),
            P(None, "mp"),
            P(None, "mp"),
            P(None, "mp"),
            P(None, "mp"),
            P("mp", None),
            P(None, "mp"),
            P("mp", None),
            P(None, "mp"),
            P(None, "mp"),
        ),
        check_vma=False,
    )
```

```python
import functools

import jax
import jax.numpy as jnp
import numpy as np
from jax import lax
from jax.experimental import pallas as pl
from jax.experimental.pallas import tpu as pltpu
from jax.sharding import PartitionSpec as P

HEADS = 8
KEY = 256
VAL = 512
QKV = 2 * KEY + VAL
VMEM_BYTES = 56 << 20
SPARE_BYTES = 12 << 20

epsilon = 1e-05
group_epsilon = 0.25
key_scale = KEY ** (-0.5)
bf16, f32 = jnp.bfloat16, jnp.float32

RING = tuple(range(0, HEADS, 2)) + tuple(range(HEADS - 1, 0, -2))
BATCHES = ((0, -1, 1, -2, 2), (-3, 3), (4,))
OFFSETS = tuple(offset for batch in BATCHES for offset in batch)
FIRST = (0, 5, 7)


def contract(left_side, right_side, left_dim, right_dim):
    return lax.dot_general(
        left_side,
        right_side,
        (((left_dim,), (right_dim,)), ((), ())),
        preferred_element_type=f32,
    )


def after(value, *earlier):
    return lax.optimization_barrier((value, *earlier))[0]


def row_stats(values):
    average = jnp.mean(values, axis=-1, keepdims=True)
    centered = values - average
    variance = jnp.mean(centered * centered, axis=-1, keepdims=True)
    return average, lax.rsqrt(variance + epsilon)


def normalize_back(grad_normed, unit_rows, inverse, norm_gain):
    scaled = grad_normed * norm_gain
    plain_mean = jnp.mean(scaled, axis=-1, keepdims=True)
    cross_mean = jnp.mean(scaled * unit_rows, axis=-1, keepdims=True)
    return inverse * (scaled - plain_mean - unit_rows * cross_mean)


def turn(values, cosine, sine):
    half = values.shape[-1] // 2
    even, odd = values[:, :half], values[:, half:]
    return jnp.concatenate([even * cosine - odd * sine, even * sine + odd * cosine], axis=1)


def sigmoid(values):
    return 1.0 / (1.0 + jnp.exp(-values))


def run(body, name, outs, scratch, *groups, late=(), flops=0, free=False):
    lists = [list(group) if isinstance(group, (list, tuple)) else [group] for group in groups]
    sizes = [len(group) for group in lists]
    values = [value for group in lists for value in group]
    fixed = len(outs) + len(scratch)

    def kernel(*refs):
        split, at = [], 0
        for size in sizes:
            split.append(refs[at : at + size])
            at += size
        sources = refs[at : at + len(late)]
        at += len(late)
        results = refs[at : at + fixed]
        at += fixed
        copies = [
            pltpu.make_async_copy(source, refs[at + i], refs[at + len(late) + i])
            for i, source in enumerate(sources)
        ]
        for copy in copies:
            copy.start()

        def fetch(i):
            def wait():
                copies[i].wait()
                return refs[at + i]

            return wait

        body(*split, *results, *[fetch(i) for i in range(len(late))])

    whole = pl.BlockSpec(memory_space=pltpu.VMEM)
    moved = sum(value.size * value.dtype.itemsize for value in (*values, *late))
    moved += sum(int(np.prod(shape)) * jnp.dtype(dtype).itemsize for shape, dtype in outs)
    held = sum(int(np.prod(shape)) * jnp.dtype(dtype).itemsize for shape, dtype in scratch)
    return pl.pallas_call(
        kernel,
        out_shape=[jax.ShapeDtypeStruct(shape, dtype) for shape, dtype in outs],
        in_specs=[whole] * len(values) + [pl.BlockSpec(memory_space=pl.ANY)] * len(late),
        out_specs=[whole] * len(outs),
        scratch_shapes=[pltpu.VMEM(shape, dtype) for shape, dtype in scratch]
        + [pltpu.VMEM(value.shape, value.dtype) for value in late]
        + [pltpu.SemaphoreType.DMA(())] * len(late),
        compiler_params=pltpu.CompilerParams(vmem_limit_bytes=min(VMEM_BYTES, moved + held + SPARE_BYTES)),
        cost_estimate=pl.CostEstimate(flops=flops, transcendentals=0, bytes_accessed=0 if free else moved),
        name=name,
    )(*values, *late)


def each_block(count, block, step):
    def body(i, unused):
        step(pl.multiple_of(i * block, block))
        return unused

    lax.fori_loop(0, count // block, body, 0)


def stage_rows(pieces, rows):
    width = rows.shape[1]
    half = pieces[0].shape[1]
    if half < width:
        rows[:, :half] = pieces[0][...]
        rows[:, half:] = pieces[1][...]
    else:
        chunk = rows.shape[0] // len(pieces)
        for at, piece in enumerate(pieces):
            rows[at * chunk : (at + 1) * chunk, :] = piece[...]


def project_body(pieces, norm, angles, tokens, normed, qkv, gate, stats, weights):
    (norm,), (angles,) = norm, angles
    stage_rows(pieces, tokens)
    count, width = normed.shape

    def normalize(first):
        span = pl.ds(first, 64)
        raw = tokens[span, :].astype(f32)
        average, inverse = row_stats(raw)
        stats[span, :] = jnp.concatenate([average, inverse], axis=1)
        value = (raw - average) * inverse * norm[0:1, :] + norm[1:2, :]
        normed[span, :] = value.astype(bf16)

    each_block(count, 64, normalize)
    weights = weights()
    half = KEY // 2
    cosine, sine = angles[:, :half], angles[:, half:]
    for part in range(2):
        raw = contract(normed[...], weights[:, part * KEY : (part + 1) * KEY], 1, 0)
        turned = turn(raw, cosine, sine)
        qkv[:, part * KEY : (part + 1) * KEY] = (turned * key_scale if part else turned).astype(bf16)
    qkv[:, 2 * KEY :] = contract(normed[...], weights[:, 2 * KEY : QKV], 1, 0).astype(bf16)
    gate[...] = contract(normed[...], weights[:, QKV:], 1, 0)


def decays(columns, rows, away, at, chunk, place, by_query):
    span = slice(at * chunk, (at + 1) * chunk)
    ids, begin = columns[span, 0:1], columns[span, 1:2]
    others, other_begin = rows[0:1, place], rows[1:2, place]
    if by_query:
        mask = (others <= ids) & (others >= begin)
        near = columns[span, 2:3]
    else:
        mask = (others >= ids) & (other_begin <= ids)
        near = columns[span, 3:4]
    return jnp.where(mask, near * away[at : at + 1, place], 0.0)


def spans_of(arrays):
    at = 0
    for array in arrays:
        yield array, slice(at, at + array.shape[0])
        at += array.shape[0]


def branch_body(own, every, gate, columns, rows, away, *refs):
    (own,), (gate,), (columns,), (rows,), (away,) = own, gate, columns, rows, away
    *parts, gated, grouped, inverse, intra, out_weight = refs
    count = own.shape[0]
    chunks = away.shape[0]
    chunk = count // chunks
    queries = own[:, :KEY]
    for array, place in spans_of(every):
        scores = contract(queries, array[:, KEY : 2 * KEY], 1, 1)
        for at in range(chunks):
            factor = decays(columns, rows, away, at, chunk, place, True)
            span = slice(at * chunk, (at + 1) * chunk)
            intra[span, place] = (scores[span] * factor).astype(bf16)
    retained = 0.0
    for array, place in spans_of(every):
        retained = retained + contract(intra[:, place], array[:, 2 * KEY :], 1, 0)
    grouped[...] = retained

    def finish(first):
        span = pl.ds(first, 64)
        value = grouped[span, :]
        average = jnp.mean(value, axis=1, keepdims=True)
        square = jnp.mean(value * value, axis=1, keepdims=True)
        scale = lax.rsqrt(square - average * average + group_epsilon)
        inverse[span, :] = scale
        value = (value - average) * scale
        grouped[span, :] = value
        pre = gate[span, :]
        gated[span, :] = (pre * sigmoid(pre) * value).astype(bf16)

    each_block(count, 64, finish)
    store_parts(parts, lambda place, weight=out_weight(): contract(gated[...], weight[:, place], 1, 0))


def store_parts(parts, product):
    first = 0
    for part in parts:
        width = part.shape[1]
        part[...] = product(slice(first, first + width)).astype(bf16)
        first += width


def feed_body(pieces, grad_pieces, rows, grad_rows, active, grad_hidden, *refs):
    *parts, work, up_weight, down_weight = refs
    stage_rows(pieces, rows)
    stage_rows(grad_pieces, grad_rows)
    up_weight = up_weight()
    work[0] = contract(rows[...], up_weight[...], 1, 0)
    work[1] = contract(grad_rows[...], down_weight()[...], 1, 1)

    def finish(first):
        span = pl.ds(first, 32)
        hidden, grad_active = work[0, span, :], work[1, span, :]
        cumulative = 0.5 * (1.0 + lax.erf(hidden * 0.7071067811865476))
        density = jnp.exp(-0.5 * hidden * hidden) * 0.3989422804014327
        active[span, :] = (hidden * cumulative).astype(bf16)
        grad_hidden[span, :] = (grad_active * (cumulative + hidden * density)).astype(bf16)

    each_block(rows.shape[0], 32, finish)
    store_parts(parts, lambda place: contract(grad_hidden[...], up_weight[place, :], 1, 1))


def down_body(active, down_weight, *parts):
    (down_weight,) = down_weight
    for value, targets in zip(active, (parts[:1], parts[1:2], parts[2:])):
        store_parts(targets, lambda place: contract(value[...], down_weight[:, place], 1, 0))


def gate_body(pieces, gate, grouped, inverse, rows, grad_gate, grad_retained, work, out_weight):
    (gate,), (grouped,), (inverse,) = gate, grouped, inverse
    stage_rows(pieces, rows)
    work[...] = contract(rows[...], out_weight()[...], 1, 1)

    def finish(first):
        span = pl.ds(first, 64)
        grad_gated, pre, value = work[span, :], gate[span, :], grouped[span, :]
        sigma = sigmoid(pre)
        grad_gate[span, :] = (grad_gated * value * (sigma * (1.0 + pre * (1.0 - sigma)))).astype(bf16)
        grads = grad_gated * (pre * sigma)
        plain = jnp.mean(grads, axis=1, keepdims=True)
        cross = jnp.mean(grads * value, axis=1, keepdims=True)
        grad_retained[span, :] = (inverse[span, :] * (grads - plain - value * cross)).astype(bf16)

    each_block(rows.shape[0], 64, finish)


def query_body(grads, every, columns, rows, away, angles, split, grad_query, plain_query):
    (grads,), (columns,), (rows,), (away,), (angles,), (split,) = grads, columns, rows, away, angles, split
    chunks = away.shape[0]
    chunk = grads.shape[0] // chunks
    total = 0.0
    for array, place in spans_of(every):
        scores = contract(grads[...], array[:, 2 * KEY :], 1, 1)
        scores = jnp.concatenate(
            [
                (
                    scores[at * chunk : (at + 1) * chunk]
                    * decays(columns, rows, away, at, chunk, place, True)
                ).astype(bf16)
                for at in range(chunks)
            ],
            axis=0,
        )
        total = total + contract(scores, array[:, KEY : 2 * KEY], 1, 0)
    half = KEY // 2
    value = turn(total, angles[:, :half], -angles[:, half:]).astype(bf16)
    grad_query[...] = value
    plain_query[...] = contract(value, split[...], 1, 1).astype(bf16)


def key_body(
    own, every, every_grad, columns, rows, away, angles, split, others, stats,
    grad_key, plain_key, grad_value, sums, *refs,
):
    (own,), (columns,), (rows,), (away,), (angles,), (split,) = own, columns, rows, away, angles, split
    (grad_query, grad_gate), (stats,) = others, stats
    *parts, work, weights, tokens = refs
    chunks = away.shape[0]
    count = own.shape[0]
    chunk = count // chunks
    total_key, total_value = 0.0, 0.0
    for (array, place), grads in zip(spans_of(every), every_grad):
        scores = contract(own[:, KEY : 2 * KEY], array[:, :KEY], 1, 1)
        grad_scores = contract(own[:, 2 * KEY :], grads[...], 1, 1)
        intra, grad_intra = [], []
        for at in range(chunks):
            factor = decays(columns, rows, away, at, chunk, place, False)
            span = slice(at * chunk, (at + 1) * chunk)
            intra.append((scores[span] * factor).astype(bf16))
            grad_intra.append((grad_scores[span] * factor).astype(bf16))
        total_value = total_value + contract(jnp.concatenate(intra, axis=0), grads[...], 1, 0)
        total_key = total_key + contract(jnp.concatenate(grad_intra, axis=0), array[:, :KEY], 1, 0)
    half = KEY // 2
    value = (turn(total_key, angles[:, :half], -angles[:, half:]) * key_scale).astype(bf16)
    grad_key[...] = value
    plain_key[...] = contract(value, split[...], 1, 1).astype(bf16)
    grad_value[...] = total_value.astype(bf16)
    work[:, :KEY] = grad_query[...]
    work[:, KEY : 2 * KEY] = value
    work[:, 2 * KEY : QKV] = grad_value[...]
    work[:, QKV:] = grad_gate[...]
    average, inverse = stats[:, 0:1], stats[:, 1:2]
    weights, tokens = weights(), tokens()
    tile = 512
    first = 0
    for part in parts:
        for at in range(0, part.shape[1], tile):
            place = slice(first + at, first + at + tile)
            value = contract(work[...], weights[place, :], 1, 1)
            part[:, at : at + tile] = value.astype(bf16)
            unit = (tokens[:, place].astype(f32) - average) * inverse
            sums[0:1, place] = jnp.sum(value * unit, axis=0, keepdims=True)
            sums[1:2, place] = jnp.sum(value, axis=0, keepdims=True)
        first += part.shape[1]


def relay_body(arrived, parts, forth, back, *, firsts):
    got_forth, got_back = arrived
    chunk, width = forth.shape[0] // len(parts), forth.shape[1]
    half = width // 2
    for at, part in enumerate(parts):
        span = slice(at * chunk, (at + 1) * chunk)
        if firsts is None:
            forth[span, :half] = (part[chunk:, :half].astype(f32) + got_forth[span, :].astype(f32)).astype(bf16)
            forth[span, half:] = part[chunk:, half:]
            back[span, :half] = part[:chunk, :half]
            back[span, half:] = (part[:chunk, half:].astype(f32) + got_back[span, :].astype(f32)).astype(bf16)
        else:
            for target, got, first in ((forth, got_forth, firsts[0]), (back, got_back, firsts[1])):
                value = part[first * chunk : (first + 1) * chunk, :].astype(f32) + got[span, :].astype(f32)
                target[span, :] = value.astype(bf16)


def finish_feed_body(values, up_grad, down_grad):
    total = values[0][...].astype(f32)
    for value in values[1:]:
        total = total + value[...].astype(f32)
    units = up_grad.shape[1]
    up_grad[...] = total[:, :units]
    down_grad[...] = total[:, units:].T


def product_shard(wide, groups, ranks, spot, arrived, left_sharded):
    cuts = [group[0].shape[1] // ranks for group in groups]
    width = wide[0].shape[1]
    if any(cut % 128 for cut in cuts):
        columns = [
            jnp.concatenate([lax.dynamic_slice_in_dim(batch, spot * cut, cut, 1) for batch in group], axis=0)
            for group, cut in zip(groups, cuts)
        ]
        columns, wide = jnp.concatenate(columns, axis=1), jnp.concatenate(wide, axis=0)
        total = contract(columns, wide, 0, 0) if left_sharded else contract(wide, columns, 0, 0)
        for value in arrived:
            total = total + value.astype(f32)
        return total.astype(bf16)
    steps = 4
    tile = width // steps
    count, total_cut = len(wide), sum(cuts)

    def kernel(spot_ref, *refs):
        narrow = refs[count : count + count * len(groups)]
        others, out = refs[count + count * len(groups) : -1], refs[-1]
        total = 0.0
        for i in range(count):
            columns = [narrow[g * count + i][...] for g in range(len(groups))]
            columns = columns[0] if len(columns) == 1 else jnp.concatenate(columns, axis=1)
            one = refs[i][...]
            total = total + (contract(columns, one, 0, 0) if left_sharded else contract(one, columns, 0, 0))
        for value in others:
            total = total + value[...].astype(f32)
        out[...] = total.astype(bf16)

    if left_sharded:
        shape, out_spec = (total_cut, width), pl.BlockSpec((total_cut, tile), lambda g, spot_ref: (0, g))
    else:
        shape, out_spec = (width, total_cut), pl.BlockSpec((tile, total_cut), lambda g, spot_ref: (g, 0))
    return pl.pallas_call(
        kernel,
        grid_spec=pltpu.PrefetchScalarGridSpec(
            num_scalar_prefetch=1,
            grid=(steps,),
            in_specs=[pl.BlockSpec((batch.shape[0], tile), lambda g, spot_ref: (0, g)) for batch in wide]
            + [
                pl.BlockSpec((batch.shape[0], cut), lambda g, spot_ref: (0, spot_ref[0]))
                for group, cut in zip(groups, cuts)
                for batch in group
            ]
            + [out_spec] * len(arrived),
            out_specs=out_spec,
        ),
        out_shape=jax.ShapeDtypeStruct(shape, bf16),
        compiler_params=pltpu.CompilerParams(vmem_limit_bytes=24 << 20),
        cost_estimate=pl.CostEstimate(flops=0, transcendentals=0, bytes_accessed=0),
        name="product_shard",
    )(spot.reshape(1).astype(jnp.int32), *wide, *[batch for group in groups for batch in group], *arrived)


def local(
    tokens,
    lengths,
    norm_gains,
    norm_biases,
    w_query,
    w_key,
    w_value,
    w_gate,
    w_out,
    w_up,
    w_down,
    out_grad,
):
    mp_size = lax.axis_size("mp")
    seq_size = lax.axis_size("seq")
    ranks = mp_size // HEADS
    mp_index = lax.axis_index("mp")
    head = mp_index // ranks
    rank = mp_index % ranks
    chunk, width = tokens.shape
    half = width // 2
    own_rows = chunk * HEADS
    sizes = [chunk * len(batch) for batch in BATCHES]

    def ring_shift(value, step):
        pairs = [
            (RING[k] * ranks + r, RING[(k + step) % HEADS] * ranks + r)
            for k in range(HEADS)
            for r in range(ranks)
        ]
        return lax.ppermute(value, "mp", pairs)

    def rank_shift(value, by):
        pairs = [(h * ranks + r, h * ranks + (r + by) % ranks) for h in range(HEADS) for r in range(ranks)]
        return lax.ppermute(value, "mp", pairs)

    def gather_ring(block, work=None, ready=(), hook=None):
        results = []
        hook = hook or (lambda step, pieces: None)

        swaps = []

        def use(at, pieces):
            if work:
                result, sent = work(at, after(pieces, results[-1:], swaps[:at]))
                results.append(result)
                swaps.append(sent if at == 0 else ())

        forth, back = block, block
        near = [block]
        for _ in range(2):
            forth, back = lax.optimization_barrier((ring_shift(forth, 1), ring_shift(back, -1)))
            near += [forth, back]
            hook(len(near) // 2, (forth, back))
        if callable(ready):
            ready = ready(near[1:3])
        forth, back = after((forth, back), ready)
        forth, back = lax.optimization_barrier((ring_shift(forth, 1), ring_shift(back, -1)))
        hook(3, (forth, back))
        use(0, near)
        far = [forth, back]
        left, right = after((forth[:, :half], back[:, half:]), results)
        left, right = ring_shift(left, 1), ring_shift(right, -1)
        use(1, far)
        ends = list(lax.optimization_barrier((left, right)))
        hook(4, ends)
        use(2, ends)
        return [near, far, ends], results

    def stack(values):
        return values[0] if len(values) == 1 else jnp.concatenate(values, axis=0)

    def scatter_ring(*part_of, hook=None):
        count = len(part_of)
        steps, sends = [], []

        def shift(forth, back):
            forth, back = lax.optimization_barrier((forth, back))
            sends.append((forth, back))
            forth, back = lax.optimization_barrier((ring_shift(forth, 1), ring_shift(back, -1)))
            steps.append((forth, back))
            tie = hook(len(steps), sends[-1], steps[-1]) if hook else None
            return after((forth, back), tie) if tie is not None else (forth, back)

        def relay(arrived, parts, firsts):
            shape = ((count * chunk, width), bf16)
            if firsts is not None:
                low = min(firsts) * chunk
                parts = [lax.slice_in_dim(part, low, low + 2 * chunk, axis=0) for part in parts]
                firsts = [first - min(firsts) for first in firsts]
            return run(
                functools.partial(relay_body, firsts=firsts), "relay", [shape, shape], [], arrived, parts, free=True
            )

        far = [part(2, ()) for part in part_of]
        arrived = shift(stack([value[0] for value in far]), stack([value[1] for value in far]))
        parts = [part(1, sends[0])[0] for part in part_of]
        forth, back = relay(arrived, parts, None)
        near = None
        for at in (4, 2):
            arrived = shift(forth, back)
            near = near or [part(0, sends[1])[0] for part in part_of]
            forth, back = relay(arrived, near, (at, at - 1))
        forth, back = shift(forth, back)

        def of(value, at):
            return value[at * chunk : (at + 1) * chunk].astype(f32)

        forth, back = ([of(value, i) for i in range(count)] for value in (forth, back))
        return [of(p, 0) + f + b for p, f, b in zip(near, forth, back)], steps

    def collect(shard):
        return [shard] + [rank_shift(shard, t) for t in range(1, ranks)]

    def assemble(pieces, axis):
        ordered = []
        for spot in range(ranks):
            value = pieces[0]
            for t in range(1, ranks):
                value = jnp.where((rank - t + ranks) % ranks == spot, pieces[t], value)
            ordered.append(value)
        return jnp.concatenate(ordered, axis=axis)

    def batch_of(array, at, axis=0):
        first = FIRST[at] * chunk
        return lax.slice_in_dim(array, first, first + sizes[at], axis=axis)

    with jax.named_scope("head_weights"):
        split = np.zeros((KEY, KEY), np.float32)
        for i in range(KEY // 2):
            split[2 * i, i] = 1.0
            split[2 * i + 1, KEY // 2 + i] = 1.0
        split = jnp.asarray(split, bf16)

        def separate(weight):
            return jnp.dot(weight, split, preferred_element_type=f32).astype(bf16)

        query_pieces, key_pieces = collect(w_query), collect(w_key)
        value_pieces = collect(after(w_value, query_pieces[1:]))
        gate_pieces = collect(after(w_gate, key_pieces[1:]))
        in_weights = jnp.concatenate(
            [
                separate(assemble(query_pieces, 1)),
                separate(assemble(key_pieces, 1)),
                assemble(value_pieces, 1),
                assemble(gate_pieces, 1),
            ],
            axis=1,
        )
        out_weight = assemble(collect(after(w_out, value_pieces[1:])), 0)

    with jax.named_scope("row_places"):
        table = np.zeros((HEADS, HEADS), np.int32)
        for k, h in enumerate(RING):
            for j, offset in enumerate(OFFSETS):
                table[h, j] = RING[(k + offset) % HEADS]
        sources = lax.dynamic_slice_in_dim(jnp.asarray(table), head, 1, 0)[0]
        inner = jnp.arange(chunk, dtype=jnp.int32)
        row_ids = jnp.concatenate(
            [
                (((sources * ranks + (rank - t + ranks) % ranks) * chunk)[:, None] + inner[None, :]).reshape(-1)
                for t in range(ranks)
            ]
        )
        ends = jnp.cumsum(lengths[0], dtype=jnp.int32)
        starts = ends - lengths[0]
        member = (row_ids[:, None] >= starts[None, :]) & (row_ids[:, None] < ends[None, :])
        begins = jnp.sum(jnp.where(member, starts[None, :], 0), axis=1, dtype=jnp.int32)
        position = (row_ids - begins)[:own_rows]
        frequencies = 10000.0 ** (-jnp.arange(KEY // 2).astype(f32) / (KEY // 2))
        angles = position.astype(f32)[:, None] * frequencies[None, :]
        angles = jnp.concatenate([jnp.cos(angles), jnp.sin(angles)], axis=1)
        log_decay = jnp.log(1.0 - 2.0 ** (-5.0 - head.astype(f32)))
        bases = row_ids[:own_rows:chunk]

    def away_of(array, at):
        return array[FIRST[at] : FIRST[at] + len(BATCHES[at])]

    normed_rows, own_qkv, gate_pre, stats_one = [None] * 3, [None] * 3, [None] * 3, [None] * 3
    token_rows = [None] * 3
    norm = jnp.stack([norm_gains[0], norm_biases[0]])

    placed = {}

    def ready(first):
        with jax.named_scope("row_factors"):
            ids, begin = after((row_ids, begins), first)
            away = bases[:, None] - ids[None, :]
            away_query = jnp.exp(jnp.maximum(away, 1 - chunk).astype(f32) * log_decay)
            away_key = jnp.exp(jnp.maximum(-away, 0).astype(f32) * log_decay)
            near = jnp.tile(inner.astype(f32) * log_decay, HEADS)
            columns = jnp.stack(
                [ids[:own_rows].astype(f32), begin[:own_rows].astype(f32), jnp.exp(near), jnp.exp(-near)],
                axis=1,
            )
            values = (
                [batch_of(angles, at) for at in range(3)],
                [batch_of(columns, at) for at in range(3)],
                [away_of(away_query, at) for at in range(3)],
                [away_of(away_key, at) for at in range(3)],
                jnp.stack([ids.astype(f32), begin.astype(f32)]),
                in_weights,
                norm,
            )
            names = ("angles", "columns", "away", "away_key", "rows", "weights", "norm")
            placed.update(zip(names, lax.optimization_barrier(values)))
        return tuple(placed.values())

    def project(at, pieces):
        token_rows[at], normed_rows[at], own_qkv[at], gate_pre[at], stats_one[at] = run(
            project_body,
            "project",
            [
                ((sizes[at], width), bf16),
                ((sizes[at], width), bf16),
                ((sizes[at], QKV), bf16),
                ((sizes[at], VAL), f32),
                ((sizes[at], 2), f32),
            ],
            [],
            pieces,
            placed["norm"],
            placed["angles"][at],
            late=[placed["weights"]],
            flops=2 * sizes[at] * width * (QKV + VAL),
        )
        other_qkv[at] = [rank_shift(own_qkv[at], t) for t in range(1, ranks)]
        return (own_qkv[at], out_weight) if at == 0 else own_qkv[at], other_qkv[at]

    other_qkv = [None] * 3
    with jax.named_scope("project_in"):
        token_pieces, _ = gather_ring(tokens, project, ready)
        every_qkv = own_qkv + [other_qkv[at][t] for t in range(ranks - 1) for at in range(3)]
    with jax.named_scope("gather_out_grad"):
        grad_steps = {}
        grad_pieces, _ = gather_ring(after(out_grad, token_pieces[2]), hook=grad_steps.__setitem__)
    with jax.named_scope("feed_weights"):
        up_weight = assemble(collect(after(w_up, token_pieces[2])), 1)
        down_weight = assemble(collect(after(w_down, token_pieces[2])), 0)

    grouped, inverse_group, gated_rows = [None] * 3, [None] * 3, [None] * 3

    def part_shapes(at):
        return [((sizes[at], half), bf16)] * 2 if at == 2 else [((sizes[at], width), bf16)]

    def branch_part(at, earlier):
        *part, gated_rows[at], grouped[at], inverse_group[at] = run(
            branch_body,
            "branch",
            part_shapes(at)
            + [
                ((sizes[at], VAL), bf16),
                ((sizes[at], VAL), f32),
                ((sizes[at], 1), f32),
            ],
            [((sizes[at], ranks * own_rows), bf16)],
            after(own_qkv[at], earlier, grad_steps[1] if at == 0 else ()),
            every_qkv,
            gate_pre[at],
            placed["columns"][at],
            placed["rows"],
            placed["away"][at],
            late=[out_weight],
            flops=2 * sizes[at] * (ranks * own_rows * (KEY + VAL) + VAL * width),
        )
        return part

    with jax.named_scope("retention"):
        (total,), _ = scatter_ring(branch_part)
        middle = tokens.astype(f32) + total

    def shard(left, right, left_sharded, spot):
        cuts = left if left_sharded else right
        cut = cuts.shape[1] // ranks
        piece = lax.dynamic_slice_in_dim(cuts, spot * cut, cut, 1)
        return contract(piece, right, 0, 0) if left_sharded else contract(left, piece, 0, 0)

    def send_shards(left, right, left_sharded):
        others = [shard(left, right, left_sharded, (rank + t) % ranks).astype(bf16) for t in range(1, ranks)]
        return others, [rank_shift(value, t + 1) for t, value in enumerate(others)]

    def own_shard(left, right, left_sharded, arrived):
        result = shard(left, right, left_sharded, rank)
        for value in arrived:
            result = result + value.astype(f32)
        return result.astype(bf16)

    def send_groups(value):
        return [
            lax.ppermute(value, "seq", [(i, (i + t) % seq_size) for i in range(seq_size)])
            for t in range(1, seq_size)
        ]

    def sum_of(value, arrived, *late):
        return sum(one.astype(f32) for one in (value, *after(arrived, *late)))

    def joined(batches):
        return jnp.concatenate(batches, axis=0)

    def by_rank(*values):
        cuts = [value.shape[1] // ranks for value in values]
        return jnp.concatenate(
            [value[:, r * cut : (r + 1) * cut] for r in range(ranks) for value, cut in zip(values, cuts)], axis=1
        )

    with jax.named_scope("norm_two"):
        average, inverse_two = row_stats(middle)
        unit_two = (middle - average) * inverse_two
        normed_two = (unit_two * norm_gains[1] + norm_biases[1]).astype(bf16)
    up_parts, two_rows, grad_rows = [None] * 3, [None] * 3, [None] * 3
    active_rows, grad_hidden_rows = [None] * 3, [None] * 3

    def feed(at, pieces):
        two_rows[at], grad_rows[at], active_rows[at], grad_hidden_rows[at], *up_parts[at] = run(
            feed_body,
            "feed",
            [
                ((sizes[at], width), bf16),
                ((sizes[at], width), bf16),
                ((sizes[at], VAL), bf16),
                ((sizes[at], VAL), bf16),
            ]
            + part_shapes(at),
            [((2, sizes[at], VAL), f32)],
            pieces,
            grad_pieces[at],
            late=[up_weight, down_weight],
            flops=6 * sizes[at] * width * VAL,
        )
        return active_rows[at], ()

    with jax.named_scope("feed_forward"):
        gather_ring(normed_two, feed)
    early = {}

    def up_hook(step, sends, arrived):
        if step == 1:
            with jax.named_scope("down_grad"):
                left, right = joined(after(grad_rows, sends)), joined(after(active_rows, sends))
                others, got = send_shards(left, right, False)
                early["down"] = own_shard(left, right, False, got)
        if step == 2:
            with jax.named_scope("up_grad"):
                left, right = joined(after(two_rows, sends)), joined(after(grad_hidden_rows, sends))
                others, got = send_shards(left, right, False)
                early["up"] = jnp.concatenate(
                    [own_shard(left, right, False, got), early["down"]], axis=1
                )
        if step == 3:
            with jax.named_scope("down_parts"):
                *parts, left, right = run(
                    down_body,
                    "down",
                    [((size, width), bf16) for size in sizes[:2]] + [((sizes[2], half), bf16)] * 2,
                    [],
                    after(active_rows, sends),
                    down_weight,
                    flops=2 * own_rows * width * VAL,
                )
                early["parts"] = [[value] for value in parts] + [[left, right]]

    with jax.named_scope("scatter_up"):
        (grad_normed_two,), up_steps = scatter_ring(lambda at, earlier: up_parts[at], hook=up_hook)
    feed_own, down_parts = early["up"], early["parts"]
    with jax.named_scope("norm_two_back"):
        grad_middle = out_grad.astype(f32) + normalize_back(
            grad_normed_two, unit_two, inverse_two, norm_gains[1]
        )
        grad_branch = grad_middle.astype(bf16)
        gain_two = jnp.sum(grad_normed_two * unit_two, axis=0)
        bias_two = jnp.sum(grad_normed_two, axis=0)

    branch_rows, grad_gate, own_grad = [None] * 3, [None] * 3, [None] * 3
    grad_query, plain_query = [None] * 3, [None] * 3

    def gate_back(at, pieces):
        branch_rows[at], grad_gate[at], own_grad[at] = run(
            gate_body,
            "gate_back",
            [
                ((sizes[at], width), bf16),
                ((sizes[at], VAL), bf16),
                ((sizes[at], VAL), bf16),
            ],
            [((sizes[at], VAL), f32)],
            pieces,
            gate_pre[at],
            grouped[at],
            inverse_group[at],
            late=[out_weight],
            flops=2 * sizes[at] * width * VAL,
        )
        other_grad[at] = [rank_shift(own_grad[at], t) for t in range(1, ranks)]
        return own_grad[at], other_grad[at]

    other_grad = [None] * 3
    with jax.named_scope("gate_back"):
        branch_pieces, _ = gather_ring(after(grad_branch, feed_own, down_parts), gate_back)
        every_grad = own_grad + [other_grad[at][t] for t in range(ranks - 1) for at in range(3)]
    with jax.named_scope("feed_grads"):
        feed_got = send_groups(feed_own)

    def query_back(at, earlier):
        with jax.named_scope("query_back"):
            grad_query[at], plain_query[at] = run(
                query_body,
                "query_back",
                [((sizes[at], KEY), bf16)] * 2,
                [],
                after(own_grad[at], earlier),
                every_qkv,
                placed["columns"][at],
                placed["rows"],
                placed["away"][at],
                placed["angles"][at],
                split,
                free=True,
            )

    def other_shards(wide, groups, left_sharded):
        others = [
            product_shard(wide, groups, ranks, (rank + t) % ranks, (), left_sharded) for t in range(1, ranks)
        ]
        return others, [rank_shift(value, t + 1) for t, value in enumerate(others)]

    with jax.named_scope("out_grad"):
        out_others, out_got = other_shards(branch_rows, [gated_rows], True)
    late_own = {}
    grad_value, plain_key = [None] * 3, [None] * 3
    norm_sums = []
    out_exchange, gate_exchange = [], []

    def in_part(at, earlier):
        query_back(at, earlier or out_others)
        if at == 2:
            with jax.named_scope("out_grad"):
                wide = after(branch_rows, grad_query[at], feed_got)
                earlier = late_own["out"] = product_shard(wide, [gated_rows], ranks, rank, out_got, True)
                out_exchange.extend(send_groups(earlier))
        if at == 1:
            with jax.named_scope("gate_grad"):
                _, late_own["got"] = other_shards(after(normed_rows, earlier), [grad_gate], False)
        if at == 0:
            with jax.named_scope("gate_grad"):
                wide = after(normed_rows, earlier)
                late_own["gate"] = product_shard(wide, [grad_gate], ranks, rank, late_own["got"], False)
        _, plain_key[at], grad_value[at], sums, *part = run(
            key_body,
            "key_back",
            [
                ((sizes[at], KEY), bf16),
                ((sizes[at], KEY), bf16),
                ((sizes[at], VAL), bf16),
                ((2, width), f32),
            ]
            + part_shapes(at),
            [((sizes[at], QKV + VAL), bf16)],
            after(own_qkv[at], earlier, late_own["gate"] if at == 0 else ()),
            every_qkv,
            every_grad,
            placed["columns"][at],
            placed["rows"],
            placed["away_key"][at],
            placed["angles"][at],
            split,
            [grad_query[at], grad_gate[at]],
            stats_one[at],
            late=[placed["weights"], token_rows[at]],
            free=True,
        )
        norm_sums.append(sums)
        return part

    with jax.named_scope("key_back"):
        def in_hook(step, sends, arrived):
            if step == 2:
                return out_exchange
            if step != 3:
                return None
            for name, groups in (("value", [grad_value]), ("query_key", [plain_query, plain_key])):
                with jax.named_scope(name + "_grad"):
                    _, got = other_shards(normed_rows, groups, False)
                    late_own[name] = product_shard(normed_rows, groups, ranks, rank, got, False)
            gate_exchange.extend(send_groups(late_own["gate"]))
            return late_own["value"], late_own["query_key"], gate_exchange

        (grad_normed_one, total), in_steps = scatter_ring(
            in_part, lambda at, earlier: down_parts[at], hook=in_hook
        )
        layer_out = middle + total
    with jax.named_scope("norm_one_back"):
        tokens_grad = grad_middle + normalize_back(
            grad_normed_one,
            (tokens.astype(f32) - stats_one[0][:chunk, 0:1]) * stats_one[0][:chunk, 1:2],
            stats_one[0][:chunk, 1:2],
            norm_gains[0],
        )

    def sum_groups(value):
        result = value
        for t in range(1, seq_size):
            pairs = [(i, (i + t) % seq_size) for i in range(seq_size)]
            result = result + lax.ppermute(value, "seq", pairs)
        return result

    with jax.named_scope("norm_grads"):
        gain_one, bias_one = sum(norm_sums)
        total_sums = after(jnp.stack([gain_one, gain_two, bias_one, bias_two]), in_steps[3])
        total = total_sums
        for t in range(1, ranks):
            total = total + rank_shift(total_sums, t)
        for bit in (1, 2, 4):
            pairs = [(h * ranks + r, (h ^ bit) * ranks + r) for h in range(HEADS) for r in range(ranks)]
            total = total + lax.ppermute(total, "mp", pairs)
        span = width // mp_size
        mine = sum_groups(lax.dynamic_slice_in_dim(total, mp_index * span, span, 1))

    units = w_up.shape[1]
    with jax.named_scope("feed_grads"):
        if units % 128:
            feed_grads = sum_of(feed_own, feed_got, in_steps[3])
            up_grad, down_grad = feed_grads[:, :units], feed_grads[:, units:].T
        else:
            up_grad, down_grad = run(
                finish_feed_body,
                "finish_feed",
                [((width, units), f32), ((units, width), f32)],
                [],
                [feed_own, *after(feed_got, in_steps[3])],
                free=True,
            )
    with jax.named_scope("out_grad"):
        out_weight_grad = sum_of(late_own["out"], out_exchange, in_steps[3])
    with jax.named_scope("gate_grad"):
        gate_grad = sum_of(late_own["gate"], gate_exchange, in_steps[3])
    done = (mine, tokens_grad, layer_out, out_weight_grad, gate_grad, up_grad, down_grad)
    with jax.named_scope("value_grad"):
        value_grad = sum_of(late_own["value"], send_groups(late_own["value"]), done)
    with jax.named_scope("query_key_grad"):
        size = KEY // ranks
        own, got = late_own["query_key"], after(send_groups(late_own["query_key"]), value_grad)
        query_grad = sum_of(own[:, :size], [value[:, :size] for value in got])
        key_grad = sum_of(own[:, size:], [value[:, size:] for value in got])
    return (
        layer_out,
        tokens_grad,
        query_grad,
        key_grad,
        value_grad,
        gate_grad,
        out_weight_grad,
        up_grad,
        down_grad,
        mine[:2],
        mine[2:],
    )


def solution(mesh):
    return jax.shard_map(
        local,
        mesh=mesh,
        in_specs=(
            P(("seq", "mp"), None),
            P("seq", None),
            P(),
            P(),
            P(None, "mp"),
            P(None, "mp"),
            P(None, "mp"),
            P(None, "mp"),
            P("mp", None),
            P(None, "mp"),
            P("mp", None),
            P(("seq", "mp"), None),
        ),
        out_specs=(
            P(("seq", "mp"), None),
            P(("seq", "mp"), None),
            P(None, "mp"),
            P(None, "mp"),
            P(None, "mp"),
            P(None, "mp"),
            P("mp", None),
            P(None, "mp"),
            P("mp", None),
            P(None, "mp"),
            P(None, "mp"),
        ),
        check_vma=False,
    )
```

```python
import functools

import jax
import jax.numpy as jnp
import numpy as np
from jax import lax
from jax.experimental import pallas as pl
from jax.experimental.pallas import tpu as pltpu
from jax.sharding import PartitionSpec as P

HEADS = 8
KEY = 256
VAL = 512
QKV = 2 * KEY + VAL
VMEM_BYTES = 56 << 20
SPARE_BYTES = 12 << 20

epsilon = 1e-05
group_epsilon = 0.25
key_scale = KEY ** (-0.5)
bf16, f32 = jnp.bfloat16, jnp.float32

RING = tuple(range(0, HEADS, 2)) + tuple(range(HEADS - 1, 0, -2))
BATCHES = ((0, -1, 1, -2, 2), (-3, 3), (4,))
OFFSETS = tuple(offset for batch in BATCHES for offset in batch)
FIRST = (0, 5, 7)


def contract(left_side, right_side, left_dim, right_dim):
    return lax.dot_general(
        left_side,
        right_side,
        (((left_dim,), (right_dim,)), ((), ())),
        preferred_element_type=f32,
    )


def after(value, *earlier):
    return lax.optimization_barrier((value, *earlier))[0]


def row_stats(values):
    average = jnp.mean(values, axis=-1, keepdims=True)
    centered = values - average
    variance = jnp.mean(centered * centered, axis=-1, keepdims=True)
    return average, lax.rsqrt(variance + epsilon)


def normalize_back(grad_normed, unit_rows, inverse, norm_gain):
    scaled = grad_normed * norm_gain
    plain_mean = jnp.mean(scaled, axis=-1, keepdims=True)
    cross_mean = jnp.mean(scaled * unit_rows, axis=-1, keepdims=True)
    return inverse * (scaled - plain_mean - unit_rows * cross_mean)


def turn(values, cosine, sine):
    half = values.shape[-1] // 2
    even, odd = values[:, :half], values[:, half:]
    return jnp.concatenate([even * cosine - odd * sine, even * sine + odd * cosine], axis=1)


def sigmoid(values):
    return 1.0 / (1.0 + jnp.exp(-values))


def run(body, name, outs, scratch, *groups, late=(), flops=0, free=False):
    lists = [list(group) if isinstance(group, (list, tuple)) else [group] for group in groups]
    sizes = [len(group) for group in lists]
    values = [value for group in lists for value in group]
    fixed = len(outs) + len(scratch)

    def kernel(*refs):
        split, at = [], 0
        for size in sizes:
            split.append(refs[at : at + size])
            at += size
        sources = refs[at : at + len(late)]
        at += len(late)
        results = refs[at : at + fixed]
        at += fixed
        copies = [
            pltpu.make_async_copy(source, refs[at + i], refs[at + len(late) + i])
            for i, source in enumerate(sources)
        ]
        for copy in copies:
            copy.start()

        def fetch(i):
            def wait():
                copies[i].wait()
                return refs[at + i]

            return wait

        body(*split, *results, *[fetch(i) for i in range(len(late))])

    whole = pl.BlockSpec(memory_space=pltpu.VMEM)
    moved = sum(value.size * value.dtype.itemsize for value in (*values, *late))
    moved += sum(int(np.prod(shape)) * jnp.dtype(dtype).itemsize for shape, dtype in outs)
    held = sum(int(np.prod(shape)) * jnp.dtype(dtype).itemsize for shape, dtype in scratch)
    return pl.pallas_call(
        kernel,
        out_shape=[jax.ShapeDtypeStruct(shape, dtype) for shape, dtype in outs],
        in_specs=[whole] * len(values) + [pl.BlockSpec(memory_space=pl.ANY)] * len(late),
        out_specs=[whole] * len(outs),
        scratch_shapes=[pltpu.VMEM(shape, dtype) for shape, dtype in scratch]
        + [pltpu.VMEM(value.shape, value.dtype) for value in late]
        + [pltpu.SemaphoreType.DMA(())] * len(late),
        compiler_params=pltpu.CompilerParams(vmem_limit_bytes=min(VMEM_BYTES, moved + held + SPARE_BYTES)),
        cost_estimate=pl.CostEstimate(flops=flops, transcendentals=0, bytes_accessed=0 if free else moved),
        name=name,
    )(*values, *late)


def each_block(count, block, step):
    def body(i, unused):
        step(pl.multiple_of(i * block, block))
        return unused

    lax.fori_loop(0, count // block, body, 0)


def stage_rows(pieces, rows):
    width = rows.shape[1]
    half = pieces[0].shape[1]
    if half < width:
        rows[:, :half] = pieces[0][...]
        rows[:, half:] = pieces[1][...]
    else:
        chunk = rows.shape[0] // len(pieces)
        for at, piece in enumerate(pieces):
            rows[at * chunk : (at + 1) * chunk, :] = piece[...]


def project_body(pieces, norm, angles, tokens, normed, qkv, gate, stats, weights):
    (norm,), (angles,) = norm, angles
    stage_rows(pieces, tokens)
    count, width = normed.shape

    def normalize(first):
        span = pl.ds(first, 64)
        raw = tokens[span, :].astype(f32)
        average, inverse = row_stats(raw)
        stats[span, :] = jnp.concatenate([average, inverse], axis=1)
        value = (raw - average) * inverse * norm[0:1, :] + norm[1:2, :]
        normed[span, :] = value.astype(bf16)

    each_block(count, 64, normalize)
    weights = weights()
    half = KEY // 2
    cosine, sine = angles[:, :half], angles[:, half:]
    for part in range(2):
        raw = contract(normed[...], weights[:, part * KEY : (part + 1) * KEY], 1, 0)
        turned = turn(raw, cosine, sine)
        qkv[:, part * KEY : (part + 1) * KEY] = (turned * key_scale if part else turned).astype(bf16)
    qkv[:, 2 * KEY :] = contract(normed[...], weights[:, 2 * KEY : QKV], 1, 0).astype(bf16)
    gate[...] = contract(normed[...], weights[:, QKV:], 1, 0)


def decays(columns, rows, away, at, chunk, place, by_query):
    span = slice(at * chunk, (at + 1) * chunk)
    ids, begin = columns[span, 0:1], columns[span, 1:2]
    others, other_begin = rows[0:1, place], rows[1:2, place]
    if by_query:
        mask = (others <= ids) & (others >= begin)
        near = columns[span, 2:3]
    else:
        mask = (others >= ids) & (other_begin <= ids)
        near = columns[span, 3:4]
    return jnp.where(mask, near * away[at : at + 1, place], 0.0)


def spans_of(arrays):
    at = 0
    for array in arrays:
        yield array, slice(at, at + array.shape[0])
        at += array.shape[0]


def branch_body(own, every, gate, columns, rows, away, *refs):
    (own,), (gate,), (columns,), (rows,), (away,) = own, gate, columns, rows, away
    *parts, gated, grouped, inverse, intra, out_weight = refs
    count = own.shape[0]
    chunks = away.shape[0]
    chunk = count // chunks
    queries = own[:, :KEY]
    for array, place in spans_of(every):
        scores = contract(queries, array[:, KEY : 2 * KEY], 1, 1)
        for at in range(chunks):
            factor = decays(columns, rows, away, at, chunk, place, True)
            span = slice(at * chunk, (at + 1) * chunk)
            intra[span, place] = (scores[span] * factor).astype(bf16)
    retained = 0.0
    for array, place in spans_of(every):
        retained = retained + contract(intra[:, place], array[:, 2 * KEY :], 1, 0)
    grouped[...] = retained

    def finish(first):
        span = pl.ds(first, 64)
        value = grouped[span, :]
        average = jnp.mean(value, axis=1, keepdims=True)
        square = jnp.mean(value * value, axis=1, keepdims=True)
        scale = lax.rsqrt(square - average * average + group_epsilon)
        inverse[span, :] = scale
        value = (value - average) * scale
        grouped[span, :] = value
        pre = gate[span, :]
        gated[span, :] = (pre * sigmoid(pre) * value).astype(bf16)

    each_block(count, 64, finish)
    store_parts(parts, count, lambda place, weight=out_weight(): contract(gated[...], weight[:, place], 1, 0))


def store_parts(parts, count, product):
    if parts[0].shape[0] < count:
        value = product(slice(None)).astype(bf16)
        first = 0
        for part in parts:
            part[...] = value[first : first + part.shape[0], :]
            first += part.shape[0]
        return
    first = 0
    for part in parts:
        width = part.shape[1]
        part[...] = product(slice(first, first + width)).astype(bf16)
        first += width


def feed_body(pieces, grad_pieces, rows, grad_rows, active, grad_hidden, *refs):
    *parts, work, up_weight, down_weight = refs
    stage_rows(pieces, rows)
    stage_rows(grad_pieces, grad_rows)
    up_weight = up_weight()
    work[0] = contract(rows[...], up_weight[...], 1, 0)
    work[1] = contract(grad_rows[...], down_weight()[...], 1, 1)

    def finish(first):
        span = pl.ds(first, 32)
        hidden, grad_active = work[0, span, :], work[1, span, :]
        cumulative = 0.5 * (1.0 + lax.erf(hidden * 0.7071067811865476))
        density = jnp.exp(-0.5 * hidden * hidden) * 0.3989422804014327
        active[span, :] = (hidden * cumulative).astype(bf16)
        grad_hidden[span, :] = (grad_active * (cumulative + hidden * density)).astype(bf16)

    each_block(rows.shape[0], 32, finish)
    store_parts(parts, rows.shape[0], lambda place: contract(grad_hidden[...], up_weight[place, :], 1, 1))


def down_body(active, down_weight, *parts):
    (down_weight,) = down_weight
    for value, targets in zip(active, (parts[:3], parts[3:4], parts[4:])):
        store_parts(targets, value.shape[0], lambda place: contract(value[...], down_weight[:, place], 1, 0))


def gate_body(pieces, gate, grouped, inverse, rows, grad_gate, grad_retained, work, out_weight):
    (gate,), (grouped,), (inverse,) = gate, grouped, inverse
    stage_rows(pieces, rows)
    work[...] = contract(rows[...], out_weight()[...], 1, 1)

    def finish(first):
        span = pl.ds(first, 64)
        grad_gated, pre, value = work[span, :], gate[span, :], grouped[span, :]
        sigma = sigmoid(pre)
        grad_gate[span, :] = (grad_gated * value * (sigma * (1.0 + pre * (1.0 - sigma)))).astype(bf16)
        grads = grad_gated * (pre * sigma)
        plain = jnp.mean(grads, axis=1, keepdims=True)
        cross = jnp.mean(grads * value, axis=1, keepdims=True)
        grad_retained[span, :] = (inverse[span, :] * (grads - plain - value * cross)).astype(bf16)

    each_block(rows.shape[0], 64, finish)


def query_body(grads, every, columns, rows, away, angles, split, grad_query, plain_query):
    (grads,), (columns,), (rows,), (away,), (angles,), (split,) = grads, columns, rows, away, angles, split
    chunks = away.shape[0]
    chunk = grads.shape[0] // chunks
    total = 0.0
    for array, place in spans_of(every):
        scores = contract(grads[...], array[:, 2 * KEY :], 1, 1)
        scores = jnp.concatenate(
            [
                (
                    scores[at * chunk : (at + 1) * chunk]
                    * decays(columns, rows, away, at, chunk, place, True)
                ).astype(bf16)
                for at in range(chunks)
            ],
            axis=0,
        )
        total = total + contract(scores, array[:, KEY : 2 * KEY], 1, 0)
    half = KEY // 2
    value = turn(total, angles[:, :half], -angles[:, half:]).astype(bf16)
    grad_query[...] = value
    plain_query[...] = contract(value, split[...], 1, 1).astype(bf16)


def key_body(
    own, every, every_grad, columns, rows, away, angles, split, others, stats,
    grad_key, plain_key, grad_value, sums, *refs,
):
    (own,), (columns,), (rows,), (away,), (angles,), (split,) = own, columns, rows, away, angles, split
    (grad_query, grad_gate), (stats,) = others, stats
    *parts, work, weights, tokens = refs
    chunks = away.shape[0]
    count = own.shape[0]
    chunk = count // chunks
    total_key, total_value = 0.0, 0.0
    for (array, place), grads in zip(spans_of(every), every_grad):
        scores = contract(own[:, KEY : 2 * KEY], array[:, :KEY], 1, 1)
        grad_scores = contract(own[:, 2 * KEY :], grads[...], 1, 1)
        intra, grad_intra = [], []
        for at in range(chunks):
            factor = decays(columns, rows, away, at, chunk, place, False)
            span = slice(at * chunk, (at + 1) * chunk)
            intra.append((scores[span] * factor).astype(bf16))
            grad_intra.append((grad_scores[span] * factor).astype(bf16))
        total_value = total_value + contract(jnp.concatenate(intra, axis=0), grads[...], 1, 0)
        total_key = total_key + contract(jnp.concatenate(grad_intra, axis=0), array[:, :KEY], 1, 0)
    half = KEY // 2
    value = (turn(total_key, angles[:, :half], -angles[:, half:]) * key_scale).astype(bf16)
    grad_key[...] = value
    plain_key[...] = contract(value, split[...], 1, 1).astype(bf16)
    grad_value[...] = total_value.astype(bf16)
    work[:, :KEY] = grad_query[...]
    work[:, KEY : 2 * KEY] = value
    work[:, 2 * KEY : QKV] = grad_value[...]
    work[:, QKV:] = grad_gate[...]
    average, inverse = stats[:, 0:1], stats[:, 1:2]
    weights, tokens = weights(), tokens()
    tile = 512
    by_rows = parts[0].shape[0] < count
    for at in range(0, tokens.shape[1], tile):
        place = slice(at, at + tile)
        value = contract(work[...], weights[place, :], 1, 1)
        first = 0
        for part in parts:
            if by_rows:
                part[:, place] = value[first : first + part.shape[0], :].astype(bf16)
                first += part.shape[0]
            else:
                if first <= at < first + part.shape[1]:
                    part[:, at - first : at - first + tile] = value.astype(bf16)
                first += part.shape[1]
        unit = (tokens[:, place].astype(f32) - average) * inverse
        sums[0:1, place] = jnp.sum(value * unit, axis=0, keepdims=True)
        sums[1:2, place] = jnp.sum(value, axis=0, keepdims=True)


def relay_body(arrived, parts, forth, back, *, halves):
    got_forth, got_back = arrived
    chunk, width = forth.shape[0] // len(parts), forth.shape[1]
    half = width // 2
    for at, part in enumerate(parts):
        span = slice(at * chunk, (at + 1) * chunk)
        if halves:
            forth[span, :half] = (part[chunk:, :half].astype(f32) + got_forth[span, :].astype(f32)).astype(bf16)
            forth[span, half:] = part[chunk:, half:]
            back[span, :half] = part[:chunk, :half]
            back[span, half:] = (part[:chunk, half:].astype(f32) + got_back[span, :].astype(f32)).astype(bf16)
        else:
            forth[span, :] = (part[chunk:, :].astype(f32) + got_forth[span, :].astype(f32)).astype(bf16)
            back[span, :] = (part[:chunk, :].astype(f32) + got_back[span, :].astype(f32)).astype(bf16)


def finish_feed_body(values, up_grad, down_grad):
    total = values[0][...].astype(f32)
    for value in values[1:]:
        total = total + value[...].astype(f32)
    units = up_grad.shape[1]
    up_grad[...] = total[:, :units]
    down_grad[...] = total[:, units:].T


def finish_body(values, *outs):
    first = 0
    for out in outs:
        place = slice(first, first + out.shape[1])
        total = values[0][:, place].astype(f32)
        for value in values[1:]:
            total = total + value[:, place].astype(f32)
        out[...] = total
        first += out.shape[1]


def finish_rows_body(arrived, parts, middle, tokens, stats, gain, layer_out, tokens_grad):
    (middle, grad_middle), (tokens,), (stats,), (gain,) = middle, tokens, stats, gain
    got_forth, got_back = arrived
    count = tokens.shape[0]

    def finish(first):
        span = pl.ds(first, 64)
        totals = []
        for at, part in enumerate(parts):
            here = pl.ds(first + at * count, 64)
            totals.append(
                part[span, :].astype(f32) + got_forth[here, :].astype(f32) + got_back[here, :].astype(f32)
            )
        layer_out[span, :] = middle[span, :] + totals[1]
        inverse = stats[span, 1:2]
        unit = (tokens[span, :].astype(f32) - stats[span, 0:1]) * inverse
        tokens_grad[span, :] = grad_middle[span, :] + normalize_back(totals[0], unit, inverse, gain[0:1, :])

    each_block(count, 64, finish)


def product_shard(wide, groups, ranks, spot, arrived, left_sharded):
    cuts = [group[0].shape[1] // ranks for group in groups]
    width = wide[0].shape[1]
    if any(cut % 128 for cut in cuts):
        columns = [
            jnp.concatenate([lax.dynamic_slice_in_dim(batch, spot * cut, cut, 1) for batch in group], axis=0)
            for group, cut in zip(groups, cuts)
        ]
        columns, wide = jnp.concatenate(columns, axis=1), jnp.concatenate(wide, axis=0)
        total = contract(columns, wide, 0, 0) if left_sharded else contract(wide, columns, 0, 0)
        for value in arrived:
            total = total + value.astype(f32)
        return total.astype(bf16)
    steps = 4
    tile = width // steps
    count, total_cut = len(wide), sum(cuts)

    def kernel(spot_ref, *refs):
        narrow = refs[count : count + count * len(groups)]
        others, out = refs[count + count * len(groups) : -1], refs[-1]
        total = 0.0
        for i in range(count):
            columns = [narrow[g * count + i][...] for g in range(len(groups))]
            columns = columns[0] if len(columns) == 1 else jnp.concatenate(columns, axis=1)
            one = refs[i][...]
            total = total + (contract(columns, one, 0, 0) if left_sharded else contract(one, columns, 0, 0))
        for value in others:
            total = total + value[...].astype(f32)
        out[...] = total.astype(bf16)

    if left_sharded:
        shape, out_spec = (total_cut, width), pl.BlockSpec((total_cut, tile), lambda g, spot_ref: (0, g))
    else:
        shape, out_spec = (width, total_cut), pl.BlockSpec((tile, total_cut), lambda g, spot_ref: (g, 0))
    return pl.pallas_call(
        kernel,
        grid_spec=pltpu.PrefetchScalarGridSpec(
            num_scalar_prefetch=1,
            grid=(steps,),
            in_specs=[pl.BlockSpec((batch.shape[0], tile), lambda g, spot_ref: (0, g)) for batch in wide]
            + [
                pl.BlockSpec((batch.shape[0], cut), lambda g, spot_ref: (0, spot_ref[0]))
                for group, cut in zip(groups, cuts)
                for batch in group
            ]
            + [out_spec] * len(arrived),
            out_specs=out_spec,
        ),
        out_shape=jax.ShapeDtypeStruct(shape, bf16),
        compiler_params=pltpu.CompilerParams(vmem_limit_bytes=24 << 20),
        cost_estimate=pl.CostEstimate(flops=0, transcendentals=0, bytes_accessed=0),
        name="product_shard",
    )(spot.reshape(1).astype(jnp.int32), *wide, *[batch for group in groups for batch in group], *arrived)


def local(
    tokens,
    lengths,
    norm_gains,
    norm_biases,
    w_query,
    w_key,
    w_value,
    w_gate,
    w_out,
    w_up,
    w_down,
    out_grad,
):
    mp_size = lax.axis_size("mp")
    seq_size = lax.axis_size("seq")
    ranks = mp_size // HEADS
    mp_index = lax.axis_index("mp")
    head = mp_index // ranks
    rank = mp_index % ranks
    chunk, width = tokens.shape
    half = width // 2
    own_rows = chunk * HEADS
    sizes = [chunk * len(batch) for batch in BATCHES]

    def ring_shift(value, step):
        pairs = [
            (RING[k] * ranks + r, RING[(k + step) % HEADS] * ranks + r)
            for k in range(HEADS)
            for r in range(ranks)
        ]
        return lax.ppermute(value, "mp", pairs)

    def rank_shift(value, by):
        pairs = [(h * ranks + r, h * ranks + (r + by) % ranks) for h in range(HEADS) for r in range(ranks)]
        return lax.ppermute(value, "mp", pairs)

    def gather_ring(block, work=None, ready=(), hook=None):
        results = []
        hook = hook or (lambda step, pieces: None)

        swaps = []

        def use(at, pieces):
            if work:
                result, sent = work(at, after(pieces, results[-1:], swaps[:at]))
                results.append(result)
                swaps.append(sent if at == 0 else ())

        forth, back = block, block
        near = [block]
        for _ in range(2):
            forth, back = lax.optimization_barrier((ring_shift(forth, 1), ring_shift(back, -1)))
            near += [forth, back]
            hook(len(near) // 2, (forth, back))
        if callable(ready):
            ready = ready(near[1:3])
        forth, back = after((forth, back), ready)
        forth, back = lax.optimization_barrier((ring_shift(forth, 1), ring_shift(back, -1)))
        hook(3, (forth, back))
        use(0, near)
        far = [forth, back]
        left, right = after((forth[:, :half], back[:, half:]), results)
        left, right = ring_shift(left, 1), ring_shift(right, -1)
        use(1, far)
        ends = list(lax.optimization_barrier((left, right)))
        hook(4, ends)
        use(2, ends)
        return [near, far, ends], results

    def stack(values):
        return values[0] if len(values) == 1 else jnp.concatenate(values, axis=0)

    def scatter_ring(*part_of, hook=None):
        count = len(part_of)
        steps, sends = [], []

        def shift(forth, back):
            forth, back = lax.optimization_barrier((forth, back))
            sends.append((forth, back))
            forth, back = lax.optimization_barrier((ring_shift(forth, 1), ring_shift(back, -1)))
            steps.append((forth, back))
            tie = hook(len(steps), sends[-1], steps[-1]) if hook else None
            return after((forth, back), tie) if tie is not None else (forth, back)

        def relay(arrived, parts, halves=False):
            if count == 1 and halves:
                (part,), (forth, back) = parts, arrived
                return (
                    jnp.concatenate(
                        [(part[chunk:, :half].astype(f32) + forth.astype(f32)).astype(bf16), part[chunk:, half:]],
                        axis=1,
                    ),
                    jnp.concatenate(
                        [part[:chunk, :half], (part[:chunk, half:].astype(f32) + back.astype(f32)).astype(bf16)],
                        axis=1,
                    ),
                )
            if count == 1:
                (part,), (forth, back) = parts, arrived
                return (
                    (part[chunk:].astype(f32) + forth.astype(f32)).astype(bf16),
                    (part[:chunk].astype(f32) + back.astype(f32)).astype(bf16),
                )
            shape = ((count * chunk, width), bf16)
            return run(
                functools.partial(relay_body, halves=halves), "relay", [shape, shape], [], arrived, parts, free=True
            )

        far = [part(2, ()) for part in part_of]
        arrived = shift(stack([value[0] for value in far]), stack([value[1] for value in far]))
        parts = [part(1, sends[0])[0] for part in part_of]
        forth, back = relay(arrived, parts, True)
        near = None
        for at in (2, 1):
            arrived = shift(forth, back)
            near = near or [part(0, sends[1]) for part in part_of]
            forth, back = relay(arrived, [pieces[at] for pieces in near])
        return shift(forth, back), [pieces[0] for pieces in near], steps

    def collect(shard):
        return [shard] + [rank_shift(shard, t) for t in range(1, ranks)]

    def assemble(pieces, axis):
        ordered = []
        for spot in range(ranks):
            value = pieces[0]
            for t in range(1, ranks):
                value = jnp.where((rank - t + ranks) % ranks == spot, pieces[t], value)
            ordered.append(value)
        return jnp.concatenate(ordered, axis=axis)

    def batch_of(array, at, axis=0):
        first = FIRST[at] * chunk
        return lax.slice_in_dim(array, first, first + sizes[at], axis=axis)

    with jax.named_scope("head_weights"):
        split = np.zeros((KEY, KEY), np.float32)
        for i in range(KEY // 2):
            split[2 * i, i] = 1.0
            split[2 * i + 1, KEY // 2 + i] = 1.0
        split = jnp.asarray(split, bf16)

        def separate(weight):
            return jnp.dot(weight, split, preferred_element_type=f32).astype(bf16)

        query_pieces, key_pieces = collect(w_query), collect(w_key)
        value_pieces = collect(after(w_value, query_pieces[1:]))
        gate_pieces = collect(after(w_gate, key_pieces[1:]))
        in_weights = jnp.concatenate(
            [
                separate(assemble(query_pieces, 1)),
                separate(assemble(key_pieces, 1)),
                assemble(value_pieces, 1),
                assemble(gate_pieces, 1),
            ],
            axis=1,
        )
        out_weight = assemble(collect(after(w_out, value_pieces[1:])), 0)

    with jax.named_scope("row_places"):
        table = np.zeros((HEADS, HEADS), np.int32)
        for k, h in enumerate(RING):
            for j, offset in enumerate(OFFSETS):
                table[h, j] = RING[(k + offset) % HEADS]
        sources = lax.dynamic_slice_in_dim(jnp.asarray(table), head, 1, 0)[0]
        inner = jnp.arange(chunk, dtype=jnp.int32)
        row_ids = jnp.concatenate(
            [
                (((sources * ranks + (rank - t + ranks) % ranks) * chunk)[:, None] + inner[None, :]).reshape(-1)
                for t in range(ranks)
            ]
        )
        ends = jnp.cumsum(lengths[0], dtype=jnp.int32)
        starts = ends - lengths[0]
        member = (row_ids[:, None] >= starts[None, :]) & (row_ids[:, None] < ends[None, :])
        begins = jnp.sum(jnp.where(member, starts[None, :], 0), axis=1, dtype=jnp.int32)
        position = (row_ids - begins)[:own_rows]
        frequencies = 10000.0 ** (-jnp.arange(KEY // 2).astype(f32) / (KEY // 2))
        angles = position.astype(f32)[:, None] * frequencies[None, :]
        angles = jnp.concatenate([jnp.cos(angles), jnp.sin(angles)], axis=1)
        log_decay = jnp.log(1.0 - 2.0 ** (-5.0 - head.astype(f32)))
        bases = row_ids[:own_rows:chunk]

    def away_of(array, at):
        return array[FIRST[at] : FIRST[at] + len(BATCHES[at])]

    normed_rows, own_qkv, gate_pre, stats_one = [None] * 3, [None] * 3, [None] * 3, [None] * 3
    token_rows = [None] * 3
    norm = jnp.stack([norm_gains[0], norm_biases[0]])

    placed = {}

    def ready(first):
        with jax.named_scope("row_factors"):
            ids, begin = row_ids, begins
            away = bases[:, None] - ids[None, :]
            away_query = jnp.exp(jnp.maximum(away, 1 - chunk).astype(f32) * log_decay)
            away_key = jnp.exp(jnp.maximum(-away, 0).astype(f32) * log_decay)
            near = jnp.tile(inner.astype(f32) * log_decay, HEADS)
            columns = jnp.stack(
                [ids[:own_rows].astype(f32), begin[:own_rows].astype(f32), jnp.exp(near), jnp.exp(-near)],
                axis=1,
            )
            values = (
                [batch_of(angles, at) for at in range(3)],
                [batch_of(columns, at) for at in range(3)],
                [away_of(away_query, at) for at in range(3)],
                [away_of(away_key, at) for at in range(3)],
                jnp.stack([ids.astype(f32), begin.astype(f32)]),
                in_weights,
                norm,
            )
            names = ("angles", "columns", "away", "away_key", "rows", "weights", "norm")
            placed.update(zip(names, lax.optimization_barrier(values)))
        return tuple(placed.values())

    def project(at, pieces):
        token_rows[at], normed_rows[at], own_qkv[at], gate_pre[at], stats_one[at] = run(
            project_body,
            "project",
            [
                ((sizes[at], width), bf16),
                ((sizes[at], width), bf16),
                ((sizes[at], QKV), bf16),
                ((sizes[at], VAL), f32),
                ((sizes[at], 2), f32),
            ],
            [],
            pieces,
            placed["norm"],
            placed["angles"][at],
            late=[placed["weights"]],
            flops=2 * sizes[at] * width * (QKV + VAL),
        )
        other_qkv[at] = [rank_shift(own_qkv[at], t) for t in range(1, ranks)]
        return (own_qkv[at], out_weight) if at == 0 else own_qkv[at], other_qkv[at]

    other_qkv = [None] * 3
    with jax.named_scope("project_in"):
        token_pieces, _ = gather_ring(tokens, project, ready)
        every_qkv = own_qkv + [other_qkv[at][t] for t in range(ranks - 1) for at in range(3)]
    with jax.named_scope("gather_out_grad"):
        grad_steps = {}
        grad_pieces, _ = gather_ring(after(out_grad, token_pieces[2]), hook=grad_steps.__setitem__)
    with jax.named_scope("feed_weights"):
        up_weight = assemble(collect(after(w_up, token_pieces[2])), 1)
        down_weight = assemble(collect(after(w_down, token_pieces[2])), 0)

    grouped, inverse_group, gated_rows = [None] * 3, [None] * 3, [None] * 3

    def part_shapes(at):
        if at == 0:
            return [((size, width), bf16) for size in (chunk, 2 * chunk, 2 * chunk)]
        return [((sizes[at], half), bf16)] * 2 if at == 2 else [((sizes[at], width), bf16)]

    def branch_part(at, earlier):
        *part, gated_rows[at], grouped[at], inverse_group[at] = run(
            branch_body,
            "branch",
            part_shapes(at)
            + [
                ((sizes[at], VAL), bf16),
                ((sizes[at], VAL), f32),
                ((sizes[at], 1), f32),
            ],
            [((sizes[at], ranks * own_rows), bf16)],
            after(own_qkv[at], earlier, grad_steps[1] if at == 0 else ()),
            every_qkv,
            gate_pre[at],
            placed["columns"][at],
            placed["rows"],
            placed["away"][at],
            late=[out_weight],
            flops=2 * sizes[at] * (ranks * own_rows * (KEY + VAL) + VAL * width),
        )
        return part

    with jax.named_scope("retention"):
        (forth, back), (part,), _ = scatter_ring(branch_part)
        middle = tokens.astype(f32) + (part.astype(f32) + forth.astype(f32) + back.astype(f32))

    def shard(left, right, left_sharded, spot):
        cuts = left if left_sharded else right
        cut = cuts.shape[1] // ranks
        piece = lax.dynamic_slice_in_dim(cuts, spot * cut, cut, 1)
        return contract(piece, right, 0, 0) if left_sharded else contract(left, piece, 0, 0)

    def send_shards(left, right, left_sharded):
        others = [shard(left, right, left_sharded, (rank + t) % ranks).astype(bf16) for t in range(1, ranks)]
        return others, [rank_shift(value, t + 1) for t, value in enumerate(others)]

    def own_shard(left, right, left_sharded, arrived):
        result = shard(left, right, left_sharded, rank)
        for value in arrived:
            result = result + value.astype(f32)
        return result.astype(bf16)

    def send_groups(value):
        return [
            lax.ppermute(value, "seq", [(i, (i + t) % seq_size) for i in range(seq_size)])
            for t in range(1, seq_size)
        ]

    def finish(value, arrived, widths, *late):
        outs = [((value.shape[0], size), f32) for size in widths]
        return run(finish_body, "finish", outs, [], [value, *after(arrived, *late)], free=True)

    def joined(batches):
        return jnp.concatenate(batches, axis=0)

    def by_rank(*values):
        cuts = [value.shape[1] // ranks for value in values]
        return jnp.concatenate(
            [value[:, r * cut : (r + 1) * cut] for r in range(ranks) for value, cut in zip(values, cuts)], axis=1
        )

    with jax.named_scope("norm_two"):
        average, inverse_two = row_stats(middle)
        unit_two = (middle - average) * inverse_two
        normed_two = (unit_two * norm_gains[1] + norm_biases[1]).astype(bf16)
    up_parts, two_rows, grad_rows = [None] * 3, [None] * 3, [None] * 3
    active_rows, grad_hidden_rows = [None] * 3, [None] * 3

    def feed(at, pieces):
        two_rows[at], grad_rows[at], active_rows[at], grad_hidden_rows[at], *up_parts[at] = run(
            feed_body,
            "feed",
            [
                ((sizes[at], width), bf16),
                ((sizes[at], width), bf16),
                ((sizes[at], VAL), bf16),
                ((sizes[at], VAL), bf16),
            ]
            + part_shapes(at),
            [((2, sizes[at], VAL), f32)],
            pieces,
            grad_pieces[at],
            late=[up_weight, down_weight],
            flops=6 * sizes[at] * width * VAL,
        )
        return active_rows[at], ()

    with jax.named_scope("feed_forward"):
        gather_ring(normed_two, feed)
    early = {}

    def up_hook(step, sends, arrived):
        if step == 1:
            with jax.named_scope("down_grad"):
                left, right = joined(after(grad_rows, sends)), joined(after(active_rows, sends))
                others, got = send_shards(left, right, False)
                early["down"] = own_shard(left, right, False, got)
        if step == 2:
            with jax.named_scope("up_grad"):
                left, right = joined(after(two_rows, sends)), joined(after(grad_hidden_rows, sends))
                others, got = send_shards(left, right, False)
                early["up"] = jnp.concatenate(
                    [own_shard(left, right, False, got), early["down"]], axis=1
                )
        if step == 3:
            with jax.named_scope("down_parts"):
                parts = run(
                    down_body,
                    "down",
                    part_shapes(0) + part_shapes(1) + part_shapes(2),
                    [],
                    after(active_rows, sends),
                    down_weight,
                    flops=2 * own_rows * width * VAL,
                )
                early["parts"] = [parts[:3], parts[3:4], parts[4:]]

    with jax.named_scope("scatter_up"):
        (forth, back), (part,), up_steps = scatter_ring(lambda at, earlier: up_parts[at], hook=up_hook)
        grad_normed_two = part.astype(f32) + forth.astype(f32) + back.astype(f32)
    feed_own, down_parts = early["up"], early["parts"]
    with jax.named_scope("norm_two_back"):
        grad_middle = out_grad.astype(f32) + normalize_back(
            grad_normed_two, unit_two, inverse_two, norm_gains[1]
        )
        grad_branch = grad_middle.astype(bf16)
        gain_two = jnp.sum(grad_normed_two * unit_two, axis=0)
        bias_two = jnp.sum(grad_normed_two, axis=0)

    branch_rows, grad_gate, own_grad = [None] * 3, [None] * 3, [None] * 3
    grad_query, plain_query = [None] * 3, [None] * 3

    def gate_back(at, pieces):
        branch_rows[at], grad_gate[at], own_grad[at] = run(
            gate_body,
            "gate_back",
            [
                ((sizes[at], width), bf16),
                ((sizes[at], VAL), bf16),
                ((sizes[at], VAL), bf16),
            ],
            [((sizes[at], VAL), f32)],
            pieces,
            gate_pre[at],
            grouped[at],
            inverse_group[at],
            late=[out_weight],
            flops=2 * sizes[at] * width * VAL,
        )
        other_grad[at] = [rank_shift(own_grad[at], t) for t in range(1, ranks)]
        return own_grad[at], other_grad[at]

    other_grad = [None] * 3
    with jax.named_scope("gate_back"):
        branch_pieces, _ = gather_ring(after(grad_branch, feed_own, down_parts), gate_back)
        every_grad = own_grad + [other_grad[at][t] for t in range(ranks - 1) for at in range(3)]
    with jax.named_scope("feed_grads"):
        feed_got = send_groups(feed_own)

    def query_back(at, earlier):
        with jax.named_scope("query_back"):
            grad_query[at], plain_query[at] = run(
                query_body,
                "query_back",
                [((sizes[at], KEY), bf16)] * 2,
                [],
                after(own_grad[at], earlier),
                every_qkv,
                placed["columns"][at],
                placed["rows"],
                placed["away"][at],
                placed["angles"][at],
                split,
                free=True,
            )

    def other_shards(wide, groups, left_sharded):
        others = [
            product_shard(wide, groups, ranks, (rank + t) % ranks, (), left_sharded) for t in range(1, ranks)
        ]
        return others, [rank_shift(value, t + 1) for t, value in enumerate(others)]

    with jax.named_scope("out_grad"):
        out_others, out_got = other_shards(branch_rows, [gated_rows], True)
    late_own = {}
    grad_value, plain_key = [None] * 3, [None] * 3
    norm_sums = []
    out_exchange, gate_exchange, last_exchange = [], [], {}

    def in_part(at, earlier):
        query_back(at, earlier or out_others)
        if at == 2:
            earlier = feed_got
        if at == 1:
            with jax.named_scope("out_grad"):
                wide = after(branch_rows, earlier)
                late_own["out"] = product_shard(wide, [gated_rows], ranks, rank, out_got, True)
                out_exchange.extend(send_groups(late_own["out"]))
            with jax.named_scope("gate_grad"):
                _, late_own["got"] = other_shards(after(normed_rows, earlier), [grad_gate], False)
        if at == 0:
            with jax.named_scope("gate_grad"):
                wide = after(normed_rows, earlier)
                late_own["gate"] = product_shard(wide, [grad_gate], ranks, rank, late_own["got"], False)
        _, plain_key[at], grad_value[at], sums, *part = run(
            key_body,
            "key_back",
            [
                ((sizes[at], KEY), bf16),
                ((sizes[at], KEY), bf16),
                ((sizes[at], VAL), bf16),
                ((2, width), f32),
            ]
            + part_shapes(at),
            [((sizes[at], QKV + VAL), bf16)],
            after(own_qkv[at], earlier, late_own["gate"] if at == 0 else ()),
            every_qkv,
            every_grad,
            placed["columns"][at],
            placed["rows"],
            placed["away_key"][at],
            placed["angles"][at],
            split,
            [grad_query[at], grad_gate[at]],
            stats_one[at],
            late=[placed["weights"], token_rows[at]],
            free=True,
        )
        norm_sums.append(sums)
        return part

    finished = {}

    def finish_early(late):
        units = w_up.shape[1]
        with jax.named_scope("feed_grads"):
            feed_late = after(feed_got, late)
            if units % 128:
                both = sum(value.astype(f32) for value in (feed_own, *feed_late))
                finished["up"], finished["down"] = both[:, :units], both[:, units:].T
            else:
                shapes = [((width, units), f32), ((units, width), f32)]
                finished["up"], finished["down"] = run(
                    finish_feed_body, "finish_feed", shapes, [], [feed_own, *feed_late], free=True
                )
        with jax.named_scope("out_grad"):
            (finished["out"],) = finish(late_own["out"], out_exchange, [width], late)
        return tuple(finished.values())

    with jax.named_scope("key_back"):
        def in_hook(step, sends, arrived):
            if step == 2:
                return out_exchange
            if step == 4:
                with jax.named_scope("gate_grad"):
                    (finished["gate"],) = finish(late_own["gate"], gate_exchange, [VAL // ranks], sends)
                return None
            if step != 3:
                return None
            late_own["sends"] = sends
            gate_exchange.extend(send_groups(late_own["gate"]))
            for name, groups in (("value", [grad_value]), ("query_key", [plain_query, plain_key])):
                with jax.named_scope(name + "_grad"):
                    wide = after(normed_rows, sends)
                    _, got = other_shards(wide, groups, False)
                    if name == "query_key":
                        wide = after(wide, finish_early(late_own["value"]), gate_exchange)
                    late_own[name] = product_shard(wide, groups, ranks, rank, got, False)
                    last_exchange[name] = send_groups(late_own[name])
            return late_own["value"]

        arrived, parts, in_steps = scatter_ring(in_part, lambda at, earlier: down_parts[at], hook=in_hook)
    with jax.named_scope("finish_rows"):
        layer_out, tokens_grad = run(
            finish_rows_body,
            "finish_rows",
            [((chunk, width), f32)] * 2,
            [],
            after(arrived, last_exchange["value"]),
            parts,
            [middle, grad_middle],
            tokens,
            stats_one[0][:chunk],
            placed["norm"],
            free=True,
        )

    def sum_groups(value):
        result = value
        for t in range(1, seq_size):
            pairs = [(i, (i + t) % seq_size) for i in range(seq_size)]
            result = result + lax.ppermute(value, "seq", pairs)
        return result

    with jax.named_scope("norm_grads"):
        gain_one, bias_one = sum(norm_sums)
        total = after(jnp.stack([gain_one, gain_two, bias_one, bias_two]), in_steps[3])

        def from_others(values, across):
            result = values
            for bits in across:
                pairs = [(h * ranks + r, (h ^ bits) * ranks + r) for h in range(HEADS) for r in range(ranks)]
                result = result + lax.ppermute(values, "mp", pairs)
            return result

        shared = total
        for t in range(1, ranks):
            shared = shared + rank_shift(total, t)
        total = from_others(after(shared, tokens_grad), (1, 2, 3))
        with jax.named_scope("value_grad"):
            (value_grad,) = finish(late_own["value"], last_exchange["value"], [VAL // ranks], tokens_grad)
        total = from_others(after(total, value_grad), (4,))
        span = width // mp_size
        mine = sum_groups(lax.dynamic_slice_in_dim(total, mp_index * span, span, 1))

    with jax.named_scope("query_key_grad"):
        query_grad, key_grad = finish(
            late_own["query_key"], last_exchange["query_key"], [KEY // ranks] * 2, value_grad, finished["gate"]
        )
    return (
        layer_out,
        tokens_grad,
        query_grad,
        key_grad,
        value_grad,
        finished["gate"],
        finished["out"],
        finished["up"],
        finished["down"],
        mine[:2],
        mine[2:],
    )


def solution(mesh):
    return jax.shard_map(
        local,
        mesh=mesh,
        in_specs=(
            P(("seq", "mp"), None),
            P("seq", None),
            P(),
            P(),
            P(None, "mp"),
            P(None, "mp"),
            P(None, "mp"),
            P(None, "mp"),
            P("mp", None),
            P(None, "mp"),
            P("mp", None),
            P(("seq", "mp"), None),
        ),
        out_specs=(
            P(("seq", "mp"), None),
            P(("seq", "mp"), None),
            P(None, "mp"),
            P(None, "mp"),
            P(None, "mp"),
            P(None, "mp"),
            P("mp", None),
            P(None, "mp"),
            P("mp", None),
            P(None, "mp"),
            P(None, "mp"),
        ),
        check_vma=False,
    )
```

```python
import functools

import jax
import jax.numpy as jnp
import numpy as np
from jax import lax
from jax.experimental import pallas as pl
from jax.experimental.pallas import tpu as pltpu
from jax.sharding import PartitionSpec as P

HEADS = 8
KEY = 256
VAL = 512
QKV = 2 * KEY + VAL
VMEM_BYTES = 56 << 20
SPARE_BYTES = 12 << 20

epsilon = 1e-05
group_epsilon = 0.25
key_scale = KEY ** (-0.5)
bf16, f32 = jnp.bfloat16, jnp.float32

RING = tuple(range(0, HEADS, 2)) + tuple(range(HEADS - 1, 0, -2))
BATCHES = ((0, -1, 1, -2, 2), (-3, 3), (4,))
OFFSETS = tuple(offset for batch in BATCHES for offset in batch)
FIRST = (0, 5, 7)


def contract(left_side, right_side, left_dim, right_dim):
    return lax.dot_general(
        left_side,
        right_side,
        (((left_dim,), (right_dim,)), ((), ())),
        preferred_element_type=f32,
    )


def after(value, *earlier):
    return lax.optimization_barrier((value, *earlier))[0]


def row_stats(values):
    average = jnp.mean(values, axis=-1, keepdims=True)
    centered = values - average
    variance = jnp.mean(centered * centered, axis=-1, keepdims=True)
    return average, lax.rsqrt(variance + epsilon)


def normalize_back(grad_normed, unit_rows, inverse, norm_gain):
    scaled = grad_normed * norm_gain
    plain_mean = jnp.mean(scaled, axis=-1, keepdims=True)
    cross_mean = jnp.mean(scaled * unit_rows, axis=-1, keepdims=True)
    return inverse * (scaled - plain_mean - unit_rows * cross_mean)


def turn(values, cosine, sine):
    half = values.shape[-1] // 2
    even, odd = values[:, :half], values[:, half:]
    return jnp.concatenate([even * cosine - odd * sine, even * sine + odd * cosine], axis=1)


def sigmoid(values):
    return 1.0 / (1.0 + jnp.exp(-values))


def run(body, name, outs, scratch, *groups, late=(), flops=0, free=False):
    lists = [list(group) if isinstance(group, (list, tuple)) else [group] for group in groups]
    sizes = [len(group) for group in lists]
    values = [value for group in lists for value in group]
    fixed = len(outs) + len(scratch)

    def kernel(*refs):
        split, at = [], 0
        for size in sizes:
            split.append(refs[at : at + size])
            at += size
        sources = refs[at : at + len(late)]
        at += len(late)
        results = refs[at : at + fixed]
        at += fixed
        copies = [
            pltpu.make_async_copy(source, refs[at + i], refs[at + len(late) + i])
            for i, source in enumerate(sources)
        ]
        for copy in copies:
            copy.start()

        def fetch(i):
            def wait():
                copies[i].wait()
                return refs[at + i]

            return wait

        body(*split, *results, *[fetch(i) for i in range(len(late))])

    whole = pl.BlockSpec(memory_space=pltpu.VMEM)
    moved = sum(value.size * value.dtype.itemsize for value in (*values, *late))
    moved += sum(int(np.prod(shape)) * jnp.dtype(dtype).itemsize for shape, dtype in outs)
    held = sum(int(np.prod(shape)) * jnp.dtype(dtype).itemsize for shape, dtype in scratch)
    return pl.pallas_call(
        kernel,
        out_shape=[jax.ShapeDtypeStruct(shape, dtype) for shape, dtype in outs],
        in_specs=[whole] * len(values) + [pl.BlockSpec(memory_space=pl.ANY)] * len(late),
        out_specs=[whole] * len(outs),
        scratch_shapes=[pltpu.VMEM(shape, dtype) for shape, dtype in scratch]
        + [pltpu.VMEM(value.shape, value.dtype) for value in late]
        + [pltpu.SemaphoreType.DMA(())] * len(late),
        compiler_params=pltpu.CompilerParams(vmem_limit_bytes=min(VMEM_BYTES, moved + held + SPARE_BYTES)),
        cost_estimate=pl.CostEstimate(flops=flops, transcendentals=0, bytes_accessed=0 if free else moved),
        name=name,
    )(*values, *late)


def each_block(count, block, step):
    def body(i, unused):
        step(pl.multiple_of(i * block, block))
        return unused

    lax.fori_loop(0, count // block, body, 0)


def stage_rows(pieces, rows):
    width = rows.shape[1]
    half = pieces[0].shape[1]
    if half < width:
        rows[:, :half] = pieces[0][...]
        rows[:, half:] = pieces[1][...]
    else:
        chunk = rows.shape[0] // len(pieces)
        for at, piece in enumerate(pieces):
            rows[at * chunk : (at + 1) * chunk, :] = piece[...]


def project_body(pieces, norm, angles, tokens, normed, qkv, gate, stats, weights):
    (norm,), (angles,) = norm, angles
    stage_rows(pieces, tokens)
    count, width = normed.shape

    def normalize(first):
        span = pl.ds(first, 64)
        raw = tokens[span, :].astype(f32)
        average, inverse = row_stats(raw)
        stats[span, :] = jnp.concatenate([average, inverse], axis=1)
        value = (raw - average) * inverse * norm[0:1, :] + norm[1:2, :]
        normed[span, :] = value.astype(bf16)

    each_block(count, 64, normalize)
    weights = weights()
    half = KEY // 2
    cosine, sine = angles[:, :half], angles[:, half:]
    for part in range(2):
        raw = contract(normed[...], weights[:, part * KEY : (part + 1) * KEY], 1, 0)
        turned = turn(raw, cosine, sine)
        qkv[:, part * KEY : (part + 1) * KEY] = (turned * key_scale if part else turned).astype(bf16)
    qkv[:, 2 * KEY :] = contract(normed[...], weights[:, 2 * KEY : QKV], 1, 0).astype(bf16)
    gate[...] = contract(normed[...], weights[:, QKV:], 1, 0)


def decays(columns, rows, away, at, chunk, place, by_query):
    span = slice(at * chunk, (at + 1) * chunk)
    ids, begin = columns[span, 0:1], columns[span, 1:2]
    others, other_begin = rows[0:1, place], rows[1:2, place]
    if by_query:
        mask = (others <= ids) & (others >= begin)
        near = columns[span, 2:3]
    else:
        mask = (others >= ids) & (other_begin <= ids)
        near = columns[span, 3:4]
    return jnp.where(mask, near * away[at : at + 1, place], 0.0)


def spans_of(arrays):
    at = 0
    for array in arrays:
        yield array, slice(at, at + array.shape[0])
        at += array.shape[0]


def branch_body(own, every, gate, columns, rows, away, *refs):
    (own,), (gate,), (columns,), (rows,), (away,) = own, gate, columns, rows, away
    *parts, gated, grouped, inverse, intra, out_weight = refs
    count = own.shape[0]
    chunks = away.shape[0]
    chunk = count // chunks
    queries = own[:, :KEY]
    for array, place in spans_of(every):
        scores = contract(queries, array[:, KEY : 2 * KEY], 1, 1)
        for at in range(chunks):
            factor = decays(columns, rows, away, at, chunk, place, True)
            span = slice(at * chunk, (at + 1) * chunk)
            intra[span, place] = (scores[span] * factor).astype(bf16)
    retained = 0.0
    for array, place in spans_of(every):
        retained = retained + contract(intra[:, place], array[:, 2 * KEY :], 1, 0)
    grouped[...] = retained

    def finish(first):
        span = pl.ds(first, 64)
        value = grouped[span, :]
        average = jnp.mean(value, axis=1, keepdims=True)
        square = jnp.mean(value * value, axis=1, keepdims=True)
        scale = lax.rsqrt(square - average * average + group_epsilon)
        inverse[span, :] = scale
        value = (value - average) * scale
        grouped[span, :] = value
        pre = gate[span, :]
        gated[span, :] = (pre * sigmoid(pre) * value).astype(bf16)

    each_block(count, 64, finish)
    store_parts(parts, count, lambda place, weight=out_weight(): contract(gated[...], weight[:, place], 1, 0))


def store_parts(parts, count, product):
    if parts[0].shape[0] < count:
        value = product(slice(None)).astype(bf16)
        first = 0
        for part in parts:
            part[...] = value[first : first + part.shape[0], :]
            first += part.shape[0]
        return
    first = 0
    for part in parts:
        width = part.shape[1]
        part[...] = product(slice(first, first + width)).astype(bf16)
        first += width


def feed_body(pieces, grad_pieces, rows, grad_rows, active, grad_hidden, *refs):
    *parts, work, up_weight, down_weight = refs
    stage_rows(pieces, rows)
    stage_rows(grad_pieces, grad_rows)
    up_weight = up_weight()
    work[0] = contract(rows[...], up_weight[...], 1, 0)
    work[1] = contract(grad_rows[...], down_weight()[...], 1, 1)

    def finish(first):
        span = pl.ds(first, 32)
        hidden, grad_active = work[0, span, :], work[1, span, :]
        cumulative = 0.5 * (1.0 + lax.erf(hidden * 0.7071067811865476))
        density = jnp.exp(-0.5 * hidden * hidden) * 0.3989422804014327
        active[span, :] = (hidden * cumulative).astype(bf16)
        grad_hidden[span, :] = (grad_active * (cumulative + hidden * density)).astype(bf16)

    each_block(rows.shape[0], 32, finish)
    store_parts(parts, rows.shape[0], lambda place: contract(grad_hidden[...], up_weight[place, :], 1, 1))


def down_body(active, down_weight, *parts):
    (down_weight,) = down_weight
    for value, targets in zip(active, (parts[:3], parts[3:4], parts[4:])):
        store_parts(targets, value.shape[0], lambda place: contract(value[...], down_weight[:, place], 1, 0))


def gate_body(pieces, gate, grouped, inverse, rows, grad_gate, grad_retained, work, out_weight):
    (gate,), (grouped,), (inverse,) = gate, grouped, inverse
    stage_rows(pieces, rows)
    work[...] = contract(rows[...], out_weight()[...], 1, 1)

    def finish(first):
        span = pl.ds(first, 64)
        grad_gated, pre, value = work[span, :], gate[span, :], grouped[span, :]
        sigma = sigmoid(pre)
        grad_gate[span, :] = (grad_gated * value * (sigma * (1.0 + pre * (1.0 - sigma)))).astype(bf16)
        grads = grad_gated * (pre * sigma)
        plain = jnp.mean(grads, axis=1, keepdims=True)
        cross = jnp.mean(grads * value, axis=1, keepdims=True)
        grad_retained[span, :] = (inverse[span, :] * (grads - plain - value * cross)).astype(bf16)

    each_block(rows.shape[0], 64, finish)


def query_body(grads, every, columns, rows, away, angles, split, grad_query, plain_query):
    (grads,), (columns,), (rows,), (away,), (angles,), (split,) = grads, columns, rows, away, angles, split
    chunks = away.shape[0]
    chunk = grads.shape[0] // chunks
    total = 0.0
    for array, place in spans_of(every):
        scores = contract(grads[...], array[:, 2 * KEY :], 1, 1)
        scores = jnp.concatenate(
            [
                (
                    scores[at * chunk : (at + 1) * chunk]
                    * decays(columns, rows, away, at, chunk, place, True)
                ).astype(bf16)
                for at in range(chunks)
            ],
            axis=0,
        )
        total = total + contract(scores, array[:, KEY : 2 * KEY], 1, 0)
    half = KEY // 2
    value = turn(total, angles[:, :half], -angles[:, half:]).astype(bf16)
    grad_query[...] = value
    plain_query[...] = contract(value, split[...], 1, 1).astype(bf16)


def key_body(
    own, every, every_grad, columns, rows, away, angles, split, others, stats,
    grad_key, plain_key, grad_value, sums, *refs,
):
    (own,), (columns,), (rows,), (away,), (angles,), (split,) = own, columns, rows, away, angles, split
    (grad_query, grad_gate), (stats,) = others, stats
    *parts, work, weights, tokens = refs
    chunks = away.shape[0]
    count = own.shape[0]
    chunk = count // chunks
    total_key, total_value = 0.0, 0.0
    for (array, place), grads in zip(spans_of(every), every_grad):
        scores = contract(own[:, KEY : 2 * KEY], array[:, :KEY], 1, 1)
        grad_scores = contract(own[:, 2 * KEY :], grads[...], 1, 1)
        intra, grad_intra = [], []
        for at in range(chunks):
            factor = decays(columns, rows, away, at, chunk, place, False)
            span = slice(at * chunk, (at + 1) * chunk)
            intra.append((scores[span] * factor).astype(bf16))
            grad_intra.append((grad_scores[span] * factor).astype(bf16))
        total_value = total_value + contract(jnp.concatenate(intra, axis=0), grads[...], 1, 0)
        total_key = total_key + contract(jnp.concatenate(grad_intra, axis=0), array[:, :KEY], 1, 0)
    half = KEY // 2
    value = (turn(total_key, angles[:, :half], -angles[:, half:]) * key_scale).astype(bf16)
    grad_key[...] = value
    plain_key[...] = contract(value, split[...], 1, 1).astype(bf16)
    grad_value[...] = total_value.astype(bf16)
    work[:, :KEY] = grad_query[...]
    work[:, KEY : 2 * KEY] = value
    work[:, 2 * KEY : QKV] = grad_value[...]
    work[:, QKV:] = grad_gate[...]
    average, inverse = stats[:, 0:1], stats[:, 1:2]
    weights, tokens = weights(), tokens()
    tile = 512
    by_rows = parts[0].shape[0] < count
    for at in range(0, tokens.shape[1], tile):
        place = slice(at, at + tile)
        value = contract(work[...], weights[place, :], 1, 1)
        first = 0
        for part in parts:
            if by_rows:
                part[:, place] = value[first : first + part.shape[0], :].astype(bf16)
                first += part.shape[0]
            else:
                if first <= at < first + part.shape[1]:
                    part[:, at - first : at - first + tile] = value.astype(bf16)
                first += part.shape[1]
        unit = (tokens[:, place].astype(f32) - average) * inverse
        sums[0:1, place] = jnp.sum(value * unit, axis=0, keepdims=True)
        sums[1:2, place] = jnp.sum(value, axis=0, keepdims=True)


def relay_body(arrived, parts, forth, back, *, halves):
    got_forth, got_back = arrived
    chunk, width = forth.shape[0] // len(parts), forth.shape[1]
    half = width // 2
    for at, part in enumerate(parts):
        span = slice(at * chunk, (at + 1) * chunk)
        if halves:
            forth[span, :half] = (part[chunk:, :half].astype(f32) + got_forth[span, :].astype(f32)).astype(bf16)
            forth[span, half:] = part[chunk:, half:]
            back[span, :half] = part[:chunk, :half]
            back[span, half:] = (part[:chunk, half:].astype(f32) + got_back[span, :].astype(f32)).astype(bf16)
        else:
            forth[span, :] = (part[chunk:, :].astype(f32) + got_forth[span, :].astype(f32)).astype(bf16)
            back[span, :] = (part[:chunk, :].astype(f32) + got_back[span, :].astype(f32)).astype(bf16)


def finish_feed_body(values, up_grad, down_grad):
    total = values[0][...].astype(f32)
    for value in values[1:]:
        total = total + value[...].astype(f32)
    units = up_grad.shape[1]
    up_grad[...] = total[:, :units]
    down_grad[...] = total[:, units:].T


def finish_body(values, *outs):
    first = 0
    for out in outs:
        place = slice(first, first + out.shape[1])
        total = values[0][:, place].astype(f32)
        for value in values[1:]:
            total = total + value[:, place].astype(f32)
        out[...] = total
        first += out.shape[1]


def finish_rows_body(arrived, parts, middle, tokens, stats, gain, layer_out, tokens_grad):
    (middle, grad_middle), (tokens,), (stats,), (gain,) = middle, tokens, stats, gain
    got_forth, got_back = arrived
    count = tokens.shape[0]

    def finish(first):
        span = pl.ds(first, 64)
        totals = []
        for at, part in enumerate(parts):
            here = pl.ds(first + at * count, 64)
            totals.append(
                part[span, :].astype(f32) + got_forth[here, :].astype(f32) + got_back[here, :].astype(f32)
            )
        layer_out[span, :] = middle[span, :] + totals[1]
        inverse = stats[span, 1:2]
        unit = (tokens[span, :].astype(f32) - stats[span, 0:1]) * inverse
        tokens_grad[span, :] = grad_middle[span, :] + normalize_back(totals[0], unit, inverse, gain[0:1, :])

    each_block(count, 64, finish)


def product_shard(wide, groups, ranks, spot, arrived, left_sharded):
    cuts = [group[0].shape[1] // ranks for group in groups]
    width = wide[0].shape[1]
    if any(cut % 128 for cut in cuts):
        columns = [
            jnp.concatenate([lax.dynamic_slice_in_dim(batch, spot * cut, cut, 1) for batch in group], axis=0)
            for group, cut in zip(groups, cuts)
        ]
        columns, wide = jnp.concatenate(columns, axis=1), jnp.concatenate(wide, axis=0)
        total = contract(columns, wide, 0, 0) if left_sharded else contract(wide, columns, 0, 0)
        for value in arrived:
            total = total + value.astype(f32)
        return total.astype(bf16)
    steps = 4
    tile = width // steps
    count, total_cut = len(wide), sum(cuts)

    def kernel(spot_ref, *refs):
        narrow = refs[count : count + count * len(groups)]
        others, out = refs[count + count * len(groups) : -1], refs[-1]
        total = 0.0
        for i in range(count):
            columns = [narrow[g * count + i][...] for g in range(len(groups))]
            columns = columns[0] if len(columns) == 1 else jnp.concatenate(columns, axis=1)
            one = refs[i][...]
            total = total + (contract(columns, one, 0, 0) if left_sharded else contract(one, columns, 0, 0))
        for value in others:
            total = total + value[...].astype(f32)
        out[...] = total.astype(bf16)

    if left_sharded:
        shape, out_spec = (total_cut, width), pl.BlockSpec((total_cut, tile), lambda g, spot_ref: (0, g))
    else:
        shape, out_spec = (width, total_cut), pl.BlockSpec((tile, total_cut), lambda g, spot_ref: (g, 0))
    return pl.pallas_call(
        kernel,
        grid_spec=pltpu.PrefetchScalarGridSpec(
            num_scalar_prefetch=1,
            grid=(steps,),
            in_specs=[pl.BlockSpec((batch.shape[0], tile), lambda g, spot_ref: (0, g)) for batch in wide]
            + [
                pl.BlockSpec((batch.shape[0], cut), lambda g, spot_ref: (0, spot_ref[0]))
                for group, cut in zip(groups, cuts)
                for batch in group
            ]
            + [out_spec] * len(arrived),
            out_specs=out_spec,
        ),
        out_shape=jax.ShapeDtypeStruct(shape, bf16),
        compiler_params=pltpu.CompilerParams(vmem_limit_bytes=24 << 20),
        cost_estimate=pl.CostEstimate(flops=0, transcendentals=0, bytes_accessed=0),
        name="product_shard",
    )(spot.reshape(1).astype(jnp.int32), *wide, *[batch for group in groups for batch in group], *arrived)


def local(
    tokens,
    lengths,
    norm_gains,
    norm_biases,
    w_query,
    w_key,
    w_value,
    w_gate,
    w_out,
    w_up,
    w_down,
    out_grad,
):
    mp_size = lax.axis_size("mp")
    seq_size = lax.axis_size("seq")
    ranks = mp_size // HEADS
    mp_index = lax.axis_index("mp")
    head = mp_index // ranks
    rank = mp_index % ranks
    chunk, width = tokens.shape
    half = width // 2
    own_rows = chunk * HEADS
    sizes = [chunk * len(batch) for batch in BATCHES]

    def ring_shift(value, step):
        pairs = [
            (RING[k] * ranks + r, RING[(k + step) % HEADS] * ranks + r)
            for k in range(HEADS)
            for r in range(ranks)
        ]
        return lax.ppermute(value, "mp", pairs)

    def rank_shift(value, by):
        pairs = [(h * ranks + r, h * ranks + (r + by) % ranks) for h in range(HEADS) for r in range(ranks)]
        return lax.ppermute(value, "mp", pairs)

    def gather_ring(block, work=None, ready=(), hook=None):
        results = []
        hook = hook or (lambda step, pieces: None)

        swaps = []

        def use(at, pieces):
            if work:
                result, sent = work(at, after(pieces, results[-1:], swaps[:at]))
                results.append(result)
                swaps.append(sent if at == 0 else ())

        forth, back = block, block
        near = [block]
        for _ in range(2):
            forth, back = lax.optimization_barrier((ring_shift(forth, 1), ring_shift(back, -1)))
            near += [forth, back]
            hook(len(near) // 2, (forth, back))
        if callable(ready):
            ready = ready(near[1:3])
        forth, back = after((forth, back), ready)
        forth, back = lax.optimization_barrier((ring_shift(forth, 1), ring_shift(back, -1)))
        hook(3, (forth, back))
        use(0, near)
        far = [forth, back]
        left, right = after((forth[:, :half], back[:, half:]), results)
        left, right = ring_shift(left, 1), ring_shift(right, -1)
        use(1, far)
        ends = list(lax.optimization_barrier((left, right)))
        hook(4, ends)
        use(2, ends)
        return [near, far, ends], results

    def stack(values):
        return values[0] if len(values) == 1 else jnp.concatenate(values, axis=0)

    def scatter_ring(*part_of, hook=None):
        count = len(part_of)
        steps, sends = [], []

        def shift(forth, back):
            forth, back = lax.optimization_barrier((forth, back))
            sends.append((forth, back))
            forth, back = lax.optimization_barrier((ring_shift(forth, 1), ring_shift(back, -1)))
            steps.append((forth, back))
            tie = hook(len(steps), sends[-1], steps[-1]) if hook else None
            return after((forth, back), tie) if tie is not None else (forth, back)

        def relay(arrived, parts, halves=False):
            if count == 1 and halves:
                (part,), (forth, back) = parts, arrived
                return (
                    jnp.concatenate(
                        [(part[chunk:, :half].astype(f32) + forth.astype(f32)).astype(bf16), part[chunk:, half:]],
                        axis=1,
                    ),
                    jnp.concatenate(
                        [part[:chunk, :half], (part[:chunk, half:].astype(f32) + back.astype(f32)).astype(bf16)],
                        axis=1,
                    ),
                )
            if count == 1:
                (part,), (forth, back) = parts, arrived
                return (
                    (part[chunk:].astype(f32) + forth.astype(f32)).astype(bf16),
                    (part[:chunk].astype(f32) + back.astype(f32)).astype(bf16),
                )
            shape = ((count * chunk, width), bf16)
            return run(
                functools.partial(relay_body, halves=halves), "relay", [shape, shape], [], arrived, parts, free=True
            )

        far = [part(2, ()) for part in part_of]
        arrived = shift(stack([value[0] for value in far]), stack([value[1] for value in far]))
        parts = [part(1, sends[0])[0] for part in part_of]
        forth, back = relay(arrived, parts, True)
        near = None
        for at in (2, 1):
            arrived = shift(forth, back)
            near = near or [part(0, sends[1]) for part in part_of]
            forth, back = relay(arrived, [pieces[at] for pieces in near])
        return shift(forth, back), [pieces[0] for pieces in near], steps

    def collect(shard):
        return [shard] + [rank_shift(shard, t) for t in range(1, ranks)]

    def assemble(pieces, axis):
        ordered = []
        for spot in range(ranks):
            value = pieces[0]
            for t in range(1, ranks):
                value = jnp.where((rank - t + ranks) % ranks == spot, pieces[t], value)
            ordered.append(value)
        return jnp.concatenate(ordered, axis=axis)

    def batch_of(array, at, axis=0):
        first = FIRST[at] * chunk
        return lax.slice_in_dim(array, first, first + sizes[at], axis=axis)

    with jax.named_scope("head_weights"):
        split = np.zeros((KEY, KEY), np.float32)
        for i in range(KEY // 2):
            split[2 * i, i] = 1.0
            split[2 * i + 1, KEY // 2 + i] = 1.0
        split = jnp.asarray(split, bf16)

        def separate(weight):
            return jnp.dot(weight, split, preferred_element_type=f32).astype(bf16)

        query_pieces, key_pieces = collect(w_query), collect(w_key)
        value_pieces = collect(after(w_value, query_pieces[1:]))
        gate_pieces = collect(after(w_gate, key_pieces[1:]))
        in_weights = jnp.concatenate(
            [
                separate(assemble(query_pieces, 1)),
                separate(assemble(key_pieces, 1)),
                assemble(value_pieces, 1),
                assemble(gate_pieces, 1),
            ],
            axis=1,
        )
        out_weight = assemble(collect(after(w_out, value_pieces[1:])), 0)

    with jax.named_scope("row_places"):
        table = np.zeros((HEADS, HEADS), np.int32)
        for k, h in enumerate(RING):
            for j, offset in enumerate(OFFSETS):
                table[h, j] = RING[(k + offset) % HEADS]
        sources = lax.dynamic_slice_in_dim(jnp.asarray(table), head, 1, 0)[0]
        inner = jnp.arange(chunk, dtype=jnp.int32)
        row_ids = jnp.concatenate(
            [
                (((sources * ranks + (rank - t + ranks) % ranks) * chunk)[:, None] + inner[None, :]).reshape(-1)
                for t in range(ranks)
            ]
        )
        ends = jnp.cumsum(lengths[0], dtype=jnp.int32)
        starts = ends - lengths[0]
        member = (row_ids[:, None] >= starts[None, :]) & (row_ids[:, None] < ends[None, :])
        begins = jnp.sum(jnp.where(member, starts[None, :], 0), axis=1, dtype=jnp.int32)
        position = (row_ids - begins)[:own_rows]
        frequencies = 10000.0 ** (-jnp.arange(KEY // 2).astype(f32) / (KEY // 2))
        angles = position.astype(f32)[:, None] * frequencies[None, :]
        angles = jnp.concatenate([jnp.cos(angles), jnp.sin(angles)], axis=1)
        log_decay = jnp.log(1.0 - 2.0 ** (-5.0 - head.astype(f32)))
        bases = row_ids[:own_rows:chunk]

    def away_of(array, at):
        return array[FIRST[at] : FIRST[at] + len(BATCHES[at])]

    normed_rows, own_qkv, gate_pre, stats_one = [None] * 3, [None] * 3, [None] * 3, [None] * 3
    token_rows = [None] * 3
    norm = jnp.stack([norm_gains[0], norm_biases[0]])

    placed = {}

    def ready(first):
        with jax.named_scope("row_factors"):
            ids, begin = row_ids, begins
            away = bases[:, None] - ids[None, :]
            away_query = jnp.exp(jnp.maximum(away, 1 - chunk).astype(f32) * log_decay)
            away_key = jnp.exp(jnp.maximum(-away, 0).astype(f32) * log_decay)
            near = jnp.tile(inner.astype(f32) * log_decay, HEADS)
            columns = jnp.stack(
                [ids[:own_rows].astype(f32), begin[:own_rows].astype(f32), jnp.exp(near), jnp.exp(-near)],
                axis=1,
            )
            values = (
                [batch_of(angles, at) for at in range(3)],
                [batch_of(columns, at) for at in range(3)],
                [away_of(away_query, at) for at in range(3)],
                [away_of(away_key, at) for at in range(3)],
                jnp.stack([ids.astype(f32), begin.astype(f32)]),
                in_weights,
                norm,
            )
            names = ("angles", "columns", "away", "away_key", "rows", "weights", "norm")
            placed.update(zip(names, lax.optimization_barrier(values)))
        return tuple(placed.values())

    def project(at, pieces):
        token_rows[at], normed_rows[at], own_qkv[at], gate_pre[at], stats_one[at] = run(
            project_body,
            "project",
            [
                ((sizes[at], width), bf16),
                ((sizes[at], width), bf16),
                ((sizes[at], QKV), bf16),
                ((sizes[at], VAL), f32),
                ((sizes[at], 2), f32),
            ],
            [],
            pieces,
            placed["norm"],
            placed["angles"][at],
            late=[placed["weights"]],
            flops=2 * sizes[at] * width * (QKV + VAL),
        )
        other_qkv[at] = [rank_shift(own_qkv[at], t) for t in range(1, ranks)]
        return (own_qkv[at], out_weight) if at == 0 else own_qkv[at], other_qkv[at]

    other_qkv = [None] * 3
    with jax.named_scope("project_in"):
        token_pieces, _ = gather_ring(tokens, project, ready)
        every_qkv = own_qkv + [other_qkv[at][t] for t in range(ranks - 1) for at in range(3)]
    with jax.named_scope("gather_out_grad"):
        grad_steps = {}
        grad_pieces, _ = gather_ring(after(out_grad, token_pieces[2]), hook=grad_steps.__setitem__)
    with jax.named_scope("feed_weights"):
        up_weight = assemble(collect(after(w_up, token_pieces[2])), 1)
        down_weight = assemble(collect(after(w_down, token_pieces[2])), 0)

    grouped, inverse_group, gated_rows = [None] * 3, [None] * 3, [None] * 3

    def part_shapes(at):
        if at == 0:
            return [((size, width), bf16) for size in (chunk, 2 * chunk, 2 * chunk)]
        return [((sizes[at], half), bf16)] * 2 if at == 2 else [((sizes[at], width), bf16)]

    def branch_part(at, earlier):
        *part, gated_rows[at], grouped[at], inverse_group[at] = run(
            branch_body,
            "branch",
            part_shapes(at)
            + [
                ((sizes[at], VAL), bf16),
                ((sizes[at], VAL), f32),
                ((sizes[at], 1), f32),
            ],
            [((sizes[at], ranks * own_rows), bf16)],
            after(own_qkv[at], earlier, grad_steps[1] if at == 0 else ()),
            every_qkv,
            gate_pre[at],
            placed["columns"][at],
            placed["rows"],
            placed["away"][at],
            late=[out_weight],
            flops=2 * sizes[at] * (ranks * own_rows * (KEY + VAL) + VAL * width),
        )
        return part

    with jax.named_scope("retention"):
        (forth, back), (part,), _ = scatter_ring(branch_part)
        middle = tokens.astype(f32) + (part.astype(f32) + forth.astype(f32) + back.astype(f32))

    def shard(left, right, left_sharded, spot):
        cuts = left if left_sharded else right
        cut = cuts.shape[1] // ranks
        piece = lax.dynamic_slice_in_dim(cuts, spot * cut, cut, 1)
        return contract(piece, right, 0, 0) if left_sharded else contract(left, piece, 0, 0)

    def send_shards(left, right, left_sharded):
        others = [shard(left, right, left_sharded, (rank + t) % ranks).astype(bf16) for t in range(1, ranks)]
        return others, [rank_shift(value, t + 1) for t, value in enumerate(others)]

    def own_shard(left, right, left_sharded, arrived):
        result = shard(left, right, left_sharded, rank)
        for value in arrived:
            result = result + value.astype(f32)
        return result.astype(bf16)

    def send_groups(value):
        return [
            lax.ppermute(value, "seq", [(i, (i + t) % seq_size) for i in range(seq_size)])
            for t in range(1, seq_size)
        ]

    def finish(value, arrived, widths, *late):
        outs = [((value.shape[0], size), f32) for size in widths]
        return run(finish_body, "finish", outs, [], [value, *after(arrived, *late)], free=True)

    def joined(batches):
        return jnp.concatenate(batches, axis=0)

    def by_rank(*values):
        cuts = [value.shape[1] // ranks for value in values]
        return jnp.concatenate(
            [value[:, r * cut : (r + 1) * cut] for r in range(ranks) for value, cut in zip(values, cuts)], axis=1
        )

    with jax.named_scope("norm_two"):
        average, inverse_two = row_stats(middle)
        unit_two = (middle - average) * inverse_two
        normed_two = (unit_two * norm_gains[1] + norm_biases[1]).astype(bf16)
    up_parts, two_rows, grad_rows = [None] * 3, [None] * 3, [None] * 3
    active_rows, grad_hidden_rows = [None] * 3, [None] * 3

    def feed(at, pieces):
        two_rows[at], grad_rows[at], active_rows[at], grad_hidden_rows[at], *up_parts[at] = run(
            feed_body,
            "feed",
            [
                ((sizes[at], width), bf16),
                ((sizes[at], width), bf16),
                ((sizes[at], VAL), bf16),
                ((sizes[at], VAL), bf16),
            ]
            + part_shapes(at),
            [((2, sizes[at], VAL), f32)],
            pieces,
            grad_pieces[at],
            late=[up_weight, down_weight],
            flops=6 * sizes[at] * width * VAL,
        )
        return active_rows[at], ()

    with jax.named_scope("feed_forward"):
        gather_ring(normed_two, feed)
    early = {}

    def up_hook(step, sends, arrived):
        if step == 1:
            with jax.named_scope("down_grad"):
                left, right = joined(after(grad_rows, sends)), joined(after(active_rows, sends))
                others, got = send_shards(left, right, False)
                early["down"] = own_shard(left, right, False, got)
        if step == 2:
            with jax.named_scope("up_grad"):
                left, right = joined(after(two_rows, sends)), joined(after(grad_hidden_rows, sends))
                others, got = send_shards(left, right, False)
                early["up"] = jnp.concatenate(
                    [own_shard(left, right, False, got), early["down"]], axis=1
                )
        if step == 3:
            with jax.named_scope("down_parts"):
                parts = run(
                    down_body,
                    "down",
                    part_shapes(0) + part_shapes(1) + part_shapes(2),
                    [],
                    after(active_rows, sends),
                    down_weight,
                    flops=2 * own_rows * width * VAL,
                )
                early["parts"] = [parts[:3], parts[3:4], parts[4:]]

    with jax.named_scope("scatter_up"):
        (forth, back), (part,), up_steps = scatter_ring(lambda at, earlier: up_parts[at], hook=up_hook)
        grad_normed_two = part.astype(f32) + forth.astype(f32) + back.astype(f32)
    feed_own, down_parts = early["up"], early["parts"]
    with jax.named_scope("norm_two_back"):
        grad_middle = out_grad.astype(f32) + normalize_back(
            grad_normed_two, unit_two, inverse_two, norm_gains[1]
        )
        grad_branch = grad_middle.astype(bf16)
        gain_two = jnp.sum(grad_normed_two * unit_two, axis=0)
        bias_two = jnp.sum(grad_normed_two, axis=0)

    branch_rows, grad_gate, own_grad = [None] * 3, [None] * 3, [None] * 3
    grad_query, plain_query = [None] * 3, [None] * 3

    def gate_back(at, pieces):
        branch_rows[at], grad_gate[at], own_grad[at] = run(
            gate_body,
            "gate_back",
            [
                ((sizes[at], width), bf16),
                ((sizes[at], VAL), bf16),
                ((sizes[at], VAL), bf16),
            ],
            [((sizes[at], VAL), f32)],
            pieces,
            gate_pre[at],
            grouped[at],
            inverse_group[at],
            late=[out_weight],
            flops=2 * sizes[at] * width * VAL,
        )
        other_grad[at] = [rank_shift(own_grad[at], t) for t in range(1, ranks)]
        return own_grad[at], other_grad[at]

    other_grad = [None] * 3
    with jax.named_scope("gate_back"):
        branch_pieces, _ = gather_ring(after(grad_branch, feed_own, down_parts), gate_back)
        every_grad = own_grad + [other_grad[at][t] for t in range(ranks - 1) for at in range(3)]
    with jax.named_scope("feed_grads"):
        feed_got = send_groups(feed_own)

    def query_back(at, earlier):
        with jax.named_scope("query_back"):
            grad_query[at], plain_query[at] = run(
                query_body,
                "query_back",
                [((sizes[at], KEY), bf16)] * 2,
                [],
                after(own_grad[at], earlier),
                every_qkv,
                placed["columns"][at],
                placed["rows"],
                placed["away"][at],
                placed["angles"][at],
                split,
                free=True,
            )

    def other_shards(wide, groups, left_sharded):
        others = [
            product_shard(wide, groups, ranks, (rank + t) % ranks, (), left_sharded) for t in range(1, ranks)
        ]
        return others, [rank_shift(value, t + 1) for t, value in enumerate(others)]

    with jax.named_scope("out_grad"):
        out_others, out_got = other_shards(branch_rows, [gated_rows], True)
    late_own = {}
    grad_value, plain_key = [None] * 3, [None] * 3
    norm_sums = []
    out_exchange, gate_exchange, last_exchange = [], [], {}

    def in_part(at, earlier):
        query_back(at, earlier or out_others)
        if at == 2:
            earlier = feed_got, out_got
        if at == 1:
            with jax.named_scope("out_grad"):
                wide = after(branch_rows, earlier)
                late_own["out"] = product_shard(wide, [gated_rows], ranks, rank, out_got, True)
                out_exchange.extend(send_groups(late_own["out"]))
            with jax.named_scope("gate_grad"):
                _, late_own["got"] = other_shards(after(normed_rows, earlier), [grad_gate], False)
        if at == 0:
            with jax.named_scope("gate_grad"):
                wide = after(normed_rows, earlier)
                late_own["gate"] = product_shard(wide, [grad_gate], ranks, rank, late_own["got"], False)
        _, plain_key[at], grad_value[at], sums, *part = run(
            key_body,
            "key_back",
            [
                ((sizes[at], KEY), bf16),
                ((sizes[at], KEY), bf16),
                ((sizes[at], VAL), bf16),
                ((2, width), f32),
            ]
            + part_shapes(at),
            [((sizes[at], QKV + VAL), bf16)],
            after(own_qkv[at], earlier, late_own["gate"] if at == 0 else ()),
            every_qkv,
            every_grad,
            placed["columns"][at],
            placed["rows"],
            placed["away_key"][at],
            placed["angles"][at],
            split,
            [grad_query[at], grad_gate[at]],
            stats_one[at],
            late=[placed["weights"], token_rows[at]],
            free=True,
        )
        norm_sums.append(sums)
        return part

    finished = {}

    def finish_early(late):
        units = w_up.shape[1]
        with jax.named_scope("feed_grads"):
            feed_late = after(feed_got, late)
            if units % 128:
                both = sum(value.astype(f32) for value in (feed_own, *feed_late))
                finished["up"], finished["down"] = both[:, :units], both[:, units:].T
            else:
                shapes = [((width, units), f32), ((units, width), f32)]
                finished["up"], finished["down"] = run(
                    finish_feed_body, "finish_feed", shapes, [], [feed_own, *feed_late], free=True
                )
        with jax.named_scope("out_grad"):
            (finished["out"],) = finish(late_own["out"], out_exchange, [width], late)
        return tuple(finished.values())

    with jax.named_scope("key_back"):
        def in_hook(step, sends, arrived):
            if step == 2:
                return out_exchange
            if step == 4:
                with jax.named_scope("gate_grad"):
                    (finished["gate"],) = finish(late_own["gate"], gate_exchange, [VAL // ranks], sends)
                return None
            if step != 3:
                return None
            late_own["sends"] = sends
            gate_exchange.extend(send_groups(late_own["gate"]))
            for name, groups in (("value", [grad_value]), ("query_key", [plain_query, plain_key])):
                with jax.named_scope(name + "_grad"):
                    wide = after(normed_rows, sends)
                    _, got = other_shards(wide, groups, False)
                    late_own[name] = product_shard(wide, groups, ranks, rank, got, False)
                    last_exchange[name] = send_groups(late_own[name])
            return late_own["value"], finish_early(late_own["value"]), gate_exchange

        arrived, parts, in_steps = scatter_ring(in_part, lambda at, earlier: down_parts[at], hook=in_hook)
    with jax.named_scope("finish_rows"):
        layer_out, tokens_grad = run(
            finish_rows_body,
            "finish_rows",
            [((chunk, width), f32)] * 2,
            [],
            after(arrived, last_exchange["value"]),
            parts,
            [middle, grad_middle],
            tokens,
            stats_one[0][:chunk],
            placed["norm"],
            free=True,
        )

    def sum_groups(value):
        result = value
        for t in range(1, seq_size):
            pairs = [(i, (i + t) % seq_size) for i in range(seq_size)]
            result = result + lax.ppermute(value, "seq", pairs)
        return result

    with jax.named_scope("norm_grads"):
        gain_one, bias_one = sum(norm_sums)
        total = after(jnp.stack([gain_one, gain_two, bias_one, bias_two]), in_steps[3])

        def from_others(values, across):
            result = values
            for bits in across:
                pairs = [(h * ranks + r, (h ^ bits) * ranks + r) for h in range(HEADS) for r in range(ranks)]
                result = result + lax.ppermute(values, "mp", pairs)
            return result

        shared = total
        for t in range(1, ranks):
            shared = shared + rank_shift(total, t)
        total = from_others(after(shared, tokens_grad), (1, 2, 3))
        with jax.named_scope("value_grad"):
            (value_grad,) = finish(late_own["value"], last_exchange["value"], [VAL // ranks], tokens_grad)
        total = from_others(after(total, value_grad), (4,))
        span = width // mp_size
        mine = sum_groups(lax.dynamic_slice_in_dim(total, mp_index * span, span, 1))

    with jax.named_scope("query_key_grad"):
        query_grad, key_grad = finish(
            late_own["query_key"], last_exchange["query_key"], [KEY // ranks] * 2, value_grad, finished["gate"]
        )
    return (
        layer_out,
        tokens_grad,
        query_grad,
        key_grad,
        value_grad,
        finished["gate"],
        finished["out"],
        finished["up"],
        finished["down"],
        mine[:2],
        mine[2:],
    )


def solution(mesh):
    return jax.shard_map(
        local,
        mesh=mesh,
        in_specs=(
            P(("seq", "mp"), None),
            P("seq", None),
            P(),
            P(),
            P(None, "mp"),
            P(None, "mp"),
            P(None, "mp"),
            P(None, "mp"),
            P("mp", None),
            P(None, "mp"),
            P("mp", None),
            P(("seq", "mp"), None),
        ),
        out_specs=(
            P(("seq", "mp"), None),
            P(("seq", "mp"), None),
            P(None, "mp"),
            P(None, "mp"),
            P(None, "mp"),
            P(None, "mp"),
            P("mp", None),
            P(None, "mp"),
            P("mp", None),
            P(None, "mp"),
            P(None, "mp"),
        ),
        check_vma=False,
    )
```
